32 devices in a mesh: groups: 2 (over y), ctx: 4 (over z), heads: 4 (over x, core).
Axes of the slice: x: 2, y: 2, z: 4, core: 2. Of those that a mesh axis runs over, the one named last changes fastest.
Arguments:
- ssm_input: bfloat16 [2048, 8192], P(('groups', 'ctx'), 'heads'), parts along dimension 0, may hold values from -6 to 6
- decay_log: float32 [2048, 128], P(('groups', 'ctx'), 'heads'), parts along dimension 0
- state_write: bfloat16 [2048, 128], P(('groups', 'ctx')), parts along dimension 0, may hold values from -2 to 2
- state_read: bfloat16 [2048, 128], P(('groups', 'ctx')), parts along dimension 0, may hold values from -2 to 2
- skip_scale: float32 [128], P('heads'), may hold values from 0.5 to 3
- gate_input: bfloat16 [2048, 8192], P(('groups', 'ctx'), 'heads'), parts along dimension 0, may hold values from -6 to 6
- ssm_gain: float32 [8192], P('heads'), may hold values from 0.1 to 1.9
- out_weight: bfloat16 [8192, 4096], P('heads', 'ctx'), may hold values from -0.0625 to 0.0625
- residual_in: bfloat16 [2048, 4096], P(('groups', 'ctx'), 'heads'), parts along dimension 0, may hold values from -24 to 24
- moe_gain: float32 [4096], P('heads'), may hold values from 0.1 to 1.9
- down_latent: bfloat16 [4096, 1024], P('heads'), may hold values from -0.09375 to 0.09375
- expert_up: bfloat16 [8, 1024, 2688], P('ctx', None, 'heads'), may hold values from -0.1875 to 0.1875
- expert_down: bfloat16 [8, 2688, 1024], P('ctx', 'heads'), may hold values from -0.125 to 0.125
- up_latent: bfloat16 [1024, 4096], P(None, 'heads'), may hold values from -0.1875 to 0.1875
- expert_ids: int32 [2048, 22], P(('groups', 'ctx')), parts along dimension 0, may hold values from 0 to 511, as said below
- combine_fixed: int32 [2048, 22], P(('groups', 'ctx')), parts along dimension 0, may hold values from 1 to 65535
Outputs:
- layer_out: bfloat16 [2048, 4096], P(('groups', 'ctx'), 'heads'), parts along dimension 0
The draws below stay inside these ranges and needn't reach their ends.
There are 2 independent parts, one for each index of `groups`. The reference program is written for one: setup_inputs(seed, part) draws one part's arguments, and reference() takes and returns one part's arrays. A program takes and returns all parts, laid end to end along the dimension named above; an argument that names none is the same for every part. Nothing has to cross between parts.
Inputs may be any that keep to these rules, and one draw needn't show every extreme that they name: `expert_ids`: each row names 22 different experts. No expert below 8 is named by more than 16 of the 256 tokens of one block, and in every block some expert below 8 is named by exactly 16 of them.
All inputs are finite; a program needn't handle non-finite values.
Results may differ from the reference program's by a relative error of at most 0.014.
Values may be sent and summed in bfloat16 or wider, within the bound.
No kernel may reach another device: no remote copies, remote signals or barrier semaphores. Data moves between devices by JAX's collectives and lax.ppermute only.
A program may use at most 128 MiB of HBM per device.

```python
import jax
import jax.numpy as jnp
from jax import lax

D = 4096
SCAN_HEADS = 128
P_SIZE = 64
N = 128
GRP = 1024
LAT = 1024
FFN = 2688
E = 512
TOPK = 22
TOK_CTX = 256
INNER = 8192
CAP = 16
WAVE = 8
WINDOW_TOKENS = 1024
N_HEADS = 4


def draw_decay_log(key, part):
    key_kind = jax.random.fold_in(key, 21)
    key_fast = jax.random.fold_in(key, 22)
    key_slow = jax.random.fold_in(key, 23)
    key_block = jax.random.fold_in(key, 24)
    key_rough = jax.random.fold_in(key, 25)
    position_key = jax.random.fold_in(key, 26)
    spike_key = jax.random.fold_in(key, 27)
    slow_share = 0.5
    is_slow = jax.random.uniform(key_kind, (SCAN_HEADS,)) < slow_share
    fast_rate = jnp.exp(jax.random.uniform(key_fast, (SCAN_HEADS,), jnp.float32, jnp.log(1.0 / 50.0), jnp.log(1.0 / 30.0)))
    slow_rate = jnp.exp(jax.random.uniform(key_slow, (SCAN_HEADS,), jnp.float32, jnp.log(0.2), jnp.log(0.5))) / WINDOW_TOKENS
    head_rate = jnp.where(is_slow, slow_rate, fast_rate)
    block_factor = jnp.exp(jax.random.uniform(key_block, (WINDOW_TOKENS // TOK_CTX, 1), jnp.float32, jnp.log(0.5), jnp.log(2.0)))
    block_factor = jnp.repeat(block_factor, TOK_CTX, axis=0)
    roughness = jnp.exp(jax.random.uniform(key_rough, (WINDOW_TOKENS, SCAN_HEADS), jnp.float32, jnp.log(0.5), jnp.log(2.0)))
    baseline_rate = head_rate[None, :] * block_factor * roughness
    spike_positions = jax.random.randint(position_key, (2,), 0, WINDOW_TOKENS)
    spike_length = jax.random.uniform(spike_key, (SCAN_HEADS,), jnp.float32, 0.22, 0.69)
    spike_mask = jnp.any(jnp.arange(WINDOW_TOKENS)[:, None] == spike_positions[None, :], axis=1)
    return (baseline_rate + jnp.where(spike_mask[:, None], spike_length[None, :], 0.0)).astype(jnp.float32)


def draw_residual_in(key, part):
    key_row = jax.random.fold_in(key, 31)
    key_col = jax.random.fold_in(key, 32)
    key_base = jax.random.fold_in(key, 33)
    row_scale = jnp.exp(jax.random.uniform(key_row, (WINDOW_TOKENS, 1), jnp.float32, jnp.log(0.3), jnp.log(3.0)))
    position = jnp.arange(D, dtype=jnp.float32)[None, :] / D
    col_scale = 0.5 * 4.0 ** position * jnp.exp(jax.random.uniform(key_col, (1, D), jnp.float32, jnp.log(0.7), jnp.log(1.4)))
    base_value = jax.random.normal(key_base, (WINDOW_TOKENS, D), jnp.float32)
    return jnp.clip(base_value * row_scale * col_scale, -24.0, 24.0).astype(jnp.bfloat16)


def draw_expert_ids(key, part):
    block_count = WINDOW_TOKENS // TOK_CTX
    hot_order = jax.random.permutation(jax.random.fold_in(key, 11), WAVE)
    is_hot = hot_order < max(1, WAVE // 8)
    entries = jnp.arange(WAVE * CAP)
    owner_of = entries // CAP
    copy_index = entries % CAP
    expert_range = jnp.arange(E)

    def one_block(block_key):
        key_load = jax.random.fold_in(block_key, 1)
        key_rows = jax.random.fold_in(block_key, 2)
        key_other = jax.random.fold_in(block_key, 3)
        key_shuffle = jax.random.fold_in(block_key, 4)
        load_count = jax.random.randint(key_load, (WAVE,), CAP // 8, CAP // 2 + 1)
        load_count = jnp.where(is_hot, CAP, load_count)
        is_valid = (copy_index < load_count[owner_of]).astype(jnp.int32)
        ranking = jnp.cumsum(is_valid) - 1
        row_order = jax.random.permutation(key_rows, TOK_CTX)
        target = row_order[jnp.mod(ranking, TOK_CTX)]
        member = jnp.zeros((TOK_CTX, E), jnp.int32).at[target, owner_of].add(is_valid)
        random_part = jax.random.randint(key_other, (TOK_CTX, E), 0, 2 ** 20) * E + expert_range[None, :]
        in_wave = expert_range[None, :] < WAVE
        scores = jnp.where(in_wave, jnp.where(member > 0, 2 ** 30 + expert_range[None, :], -1 - expert_range[None, :]), random_part)
        ignored, chosen = lax.top_k(scores, TOPK)
        shuffle_keys = jax.random.randint(key_shuffle, (TOK_CTX, TOPK), 0, 2 ** 20) * TOPK + jnp.arange(TOPK)[None, :]
        new_order = jnp.argsort(shuffle_keys, axis=1)
        return jnp.take_along_axis(chosen, new_order, axis=1)
    block_keys = jax.random.split(key, block_count)
    return jax.vmap(one_block)(block_keys).reshape(WINDOW_TOKENS, TOPK).astype(jnp.int32)


def place_ends(result, own_key, low, high):
    dims = result.shape
    index_at = [jax.random.randint(jax.random.fold_in(own_key, axis), (), 0, dims[axis]) for axis in range(len(dims))]
    result = result.at[tuple(index_at)].set(low)
    longest = dims.index(max(dims))
    index_at[longest] = (index_at[longest] + 1) % dims[longest]
    return result.at[tuple(index_at)].set(high)


def shard_levels(own_key, dims, cuts, smallest, largest):
    loudness = 1.0
    for dim, blocks in cuts:
        heights = jax.random.uniform(jax.random.fold_in(jax.random.fold_in(own_key, 6), dim), (blocks,), jnp.float32, smallest / len(cuts), largest / len(cuts))
        loudness = loudness * jnp.repeat(jnp.exp(heights), dims[dim] // blocks).reshape((-1,) + (1,) * (len(dims) - 1 - dim))
    return loudness


def gaussian(own_key, dims, scale, limit, cuts=(), kind=jnp.bfloat16):
    factor_of = shard_levels(own_key, dims, cuts, -0.22, 0.18) if cuts else 1.0
    values = jax.random.normal(own_key, dims, jnp.float32) * scale * factor_of
    return jnp.minimum(jnp.maximum(values, -limit), limit).astype(kind)


def setup_inputs(seed: int = 0, part: int = 0) -> dict:
    key_of = jax.random.split(jax.random.key(seed), 17)
    part_splits = jax.random.split(jax.random.fold_in(key_of[16], part), 17)
    return {
        "ssm_input": gaussian(part_splits[0], (WINDOW_TOKENS, INNER), 1.0, 6.0, ((0, 4), (1, 4))),
        "decay_log": draw_decay_log(jax.random.fold_in(jax.random.fold_in(key_of[16], part), 71), part),
        "state_write": gaussian(part_splits[2], (WINDOW_TOKENS, N), 0.3, 2.0, ((0, 4),)),
        "state_read": gaussian(part_splits[3], (WINDOW_TOKENS, N), 0.3, 2.0, ((0, 4),)),
        "skip_scale": jnp.clip(0.5 + 2.5 * jax.random.uniform(key_of[4], (SCAN_HEADS,), jnp.float32) ** shard_levels(key_of[4], (SCAN_HEADS,), ((0, 4),), -0.2, 0.2), 0.5, 3.0),
        "gate_input": gaussian(part_splits[5], (WINDOW_TOKENS, INNER), 1.0, 6.0, ((0, 4), (1, 4))),
        "ssm_gain": jnp.clip(1.0 + 0.18 * jax.random.normal(key_of[6], (INNER,), jnp.float32), 0.1, 1.9),
        "out_weight": gaussian(key_of[7], (INNER, D), INNER ** -0.5, 0.0625, ((0, 4), (1, 4))),
        "residual_in": draw_residual_in(jax.random.fold_in(jax.random.fold_in(key_of[16], part), 71), part),
        "moe_gain": jnp.clip(1.0 + 0.18 * jax.random.normal(key_of[9], (D,), jnp.float32), 0.1, 1.9),
        "down_latent": gaussian(key_of[10], (D, LAT), D ** -0.5, 0.09375, ((0, 4),)),
        "expert_up": gaussian(key_of[11], (WAVE, LAT, FFN), LAT ** -0.5, 0.1875, ((0, 4), (2, 4))),
        "expert_down": gaussian(key_of[12], (WAVE, FFN, LAT), FFN ** -0.5, 0.125, ((0, 4), (1, 4))),
        "up_latent": gaussian(key_of[13], (LAT, D), LAT ** -0.5, 0.1875, ((1, 4),)),
        "expert_ids": draw_expert_ids(jax.random.fold_in(jax.random.fold_in(key_of[16], part), 71), part),
        "combine_fixed": place_ends(jax.random.randint(part_splits[15], (WINDOW_TOKENS, TOPK), 1, 65536), jax.random.fold_in(part_splits[15], 1), 1, 65535).astype(jnp.int32),
    }


epsilon = 1e-05

def ssd_block(carry_state, block_data):
    inputs, decays, writes, reads, writes_low, reads_low = block_data
    cumulative = jnp.cumsum(decays, axis=0)
    length_tok = inputs.shape[0]
    causal = jnp.arange(length_tok)[:, None] >= jnp.arange(length_tok)[None, :]
    spread = jnp.where(causal[:, :, None], cumulative[:, None, :] - cumulative[None, :, :], 0.0)
    intersection = jnp.dot(reads_low, writes_low.T, preferred_element_type=jnp.float32)
    mixing = jnp.where(causal[:, :, None], jnp.exp(-spread), 0.0) * intersection[:, :, None]
    within = jnp.einsum('tsh,shp->thp', mixing, inputs, precision=lax.Precision.HIGHEST)
    carried = jnp.einsum('tn,hnp->thp', reads, carry_state, precision=lax.Precision.HIGHEST) * jnp.exp(-cumulative)[:, :, None]
    tail_decay = jnp.exp(cumulative - cumulative[-1][None, :])
    fresh = jnp.einsum('sn,sh,shp->hnp', writes, tail_decay, inputs, precision=lax.Precision.HIGHEST)
    new_state = carry_state * jnp.exp(-cumulative[-1])[:, None, None] + fresh
    return (new_state, within + carried)

def rms_groups(gated, gain):
    grouped = gated.reshape(gated.shape[0], -1, GRP)
    inv_rms = lax.rsqrt(lax.optimization_barrier(jnp.mean(grouped * grouped, axis=2, keepdims=True)) + epsilon)
    return (grouped * inv_rms).reshape(gated.shape) * gain

def route_tables(ids_block, fixed_block):
    matches = ids_block[:, :, None] == jnp.arange(WAVE)[None, None, :]
    chosen = jnp.any(matches, axis=1).astype(jnp.int32)
    weight_fixed = lax.optimization_barrier(jnp.sum(jnp.where(matches, fixed_block[:, :, None], 0), axis=1))
    slot_index = jnp.cumsum(chosen, axis=0) - 1
    placed = (chosen[:, :, None] == 1) & (slot_index[:, :, None] == jnp.arange(CAP)[None, None, :])
    route_weight = (weight_fixed.astype(jnp.float32) / 65536.0).astype(jnp.bfloat16)
    table = jnp.where(placed, route_weight[:, :, None], jnp.zeros((), jnp.bfloat16)).astype(jnp.bfloat16)
    return (placed.astype(jnp.bfloat16).reshape(TOK_CTX, WAVE * CAP), table.reshape(TOK_CTX, WAVE * CAP))

def expert_apply(operands):
    rows_in, first_mat, second_mat = operands
    hidden = jnp.dot(rows_in, first_mat, preferred_element_type=jnp.float32)
    hidden = (jnp.maximum(hidden, 0.0) ** 2).astype(jnp.bfloat16)
    return jnp.dot(hidden, second_mat, preferred_element_type=jnp.float32).astype(jnp.bfloat16)

def reference(ssm_input, decay_log, state_write, state_read, skip_scale, gate_input, ssm_gain, out_weight, residual_in, moe_gain, down_latent, expert_up, expert_down, up_latent, expert_ids, combine_fixed):
    block_count = WINDOW_TOKENS // TOK_CTX
    inputs = ssm_input.astype(jnp.float32).reshape(block_count, TOK_CTX, SCAN_HEADS, P_SIZE)
    decays = decay_log.astype(jnp.float32).reshape(block_count, TOK_CTX, SCAN_HEADS)
    writes = state_write.astype(jnp.float32).reshape(block_count, TOK_CTX, N)
    reads = state_read.astype(jnp.float32).reshape(block_count, TOK_CTX, N)
    writes_low = state_write.reshape(block_count, TOK_CTX, N)
    reads_low = state_read.reshape(block_count, TOK_CTX, N)
    start_state = jnp.zeros((SCAN_HEADS, N, P_SIZE), jnp.float32)
    ignored, mixed = lax.scan(ssd_block, start_state, (inputs, decays, writes, reads, writes_low, reads_low))
    mixed = mixed.reshape(WINDOW_TOKENS, SCAN_HEADS, P_SIZE) + skip_scale[None, :, None] * inputs.reshape(WINDOW_TOKENS, SCAN_HEADS, P_SIZE)
    gated = mixed.reshape(WINDOW_TOKENS, INNER) * jax.nn.silu(gate_input.astype(jnp.float32))
    normed = rms_groups(gated, ssm_gain).astype(jnp.bfloat16)
    slice_width = INNER // N_HEADS
    mamba_out = jnp.zeros((WINDOW_TOKENS, D), jnp.float32)
    for head_slice in range(N_HEADS):
        lower = head_slice * slice_width
        partial_value = jnp.dot(normed[:, lower:lower + slice_width], out_weight[lower:lower + slice_width], preferred_element_type=jnp.float32)
        partial_value = lax.optimization_barrier(partial_value.astype(jnp.bfloat16))
        mamba_out = mamba_out + partial_value.astype(jnp.float32)
    residual = residual_in.astype(jnp.float32) + mamba_out
    inv_rms = lax.rsqrt(lax.optimization_barrier(jnp.mean(residual * residual, axis=1, keepdims=True)) + epsilon)
    scaled = (residual * moe_gain).astype(jnp.bfloat16)
    latent = (jnp.dot(scaled, down_latent, preferred_element_type=jnp.float32) * inv_rms).astype(jnp.bfloat16)
    placed, tables = jax.vmap(route_tables)(expert_ids.reshape(block_count, TOK_CTX, TOPK), combine_fixed.reshape(block_count, TOK_CTX, TOPK))
    latent_blocks = latent.reshape(block_count, TOK_CTX, LAT)
    dispatched = jax.vmap(lambda place_block, latent_block: jnp.dot(place_block.T, latent_block, preferred_element_type=jnp.float32))(placed, latent_blocks)
    dispatched = dispatched.astype(jnp.bfloat16).reshape(block_count, WAVE, CAP, LAT)
    expert_rows = dispatched.transpose(1, 0, 2, 3).reshape(WAVE, block_count * CAP, LAT)
    expert_out = lax.map(expert_apply, (expert_rows, expert_up, expert_down))
    returned = expert_out.reshape(WAVE, block_count, CAP, LAT).transpose(1, 0, 2, 3).reshape(block_count, WAVE * CAP, LAT)
    combined = jax.vmap(lambda table_block, back_block: jnp.dot(table_block, back_block, preferred_element_type=jnp.float32))(tables, returned)
    combined_low = combined.reshape(WINDOW_TOKENS, LAT).astype(jnp.bfloat16)
    moe_out = jnp.dot(combined_low, up_latent, preferred_element_type=jnp.float32)
    return (residual + moe_out).astype(jnp.bfloat16)
```

```python
import functools

import jax
import jax.numpy as jnp
from jax import lax
from jax.experimental import pallas as pl
from jax.experimental.pallas import tpu as pltpu
from jax.sharding import PartitionSpec as P

GRP = 1024
CAP = 16
EPS = 1e-05
PAD = 16
SQL = 128
BF = jnp.bfloat16
F32 = jnp.float32

VM = pl.BlockSpec(memory_space=pltpu.VMEM)
SM = pl.BlockSpec(memory_space=pltpu.SMEM)
ANY = pl.BlockSpec(memory_space=pl.ANY)


def sds(shape, dtype=BF):
    return jax.ShapeDtypeStruct(shape, dtype)


def dot(a, b):
    return jnp.dot(a, b, preferred_element_type=F32)


def split(v, terms):
    out = []
    for _ in range(terms):
        part = v.astype(BF)
        out.append(part)
        v = v - part.astype(F32)
    return out


def iota(shape, dim):
    return lax.broadcasted_iota(jnp.int32, shape, dim)


def arrivals(n):
    table = []
    for c in range(n):
        row = [("O", 0, c)]
        for s in range(1, n):
            if c - s >= 0:
                row.append(("R", s, c - s))
            if c + s < n:
                row.append(("L", s, c + s))
        table.append(row)
    return table


def state_kernel(n, heads, width, scal, x_ref, decay_ref, write_ref, cume_ref, cumt_ref, *rest):
    outs, pieces = rest[:n], rest[n]
    rows = x_ref.shape[0]
    cols = heads * width
    piece = cols // n
    c = scal[0]
    lower = (iota((rows, rows), 0) >= iota((rows, rows), 1)).astype(F32).astype(BF)
    decay = decay_ref[...]
    cum = sum(dot(lower, part) for part in split(decay, 3))
    cumt_ref[...] = cum.T
    spread = (iota((heads, cols), 1) // width == iota((heads, cols), 0)).astype(F32).astype(BF)
    cume = sum(dot(part, spread) for part in split(cum, 3))
    cume_ref[...] = cume
    last = cume[rows - 1 : rows, :]
    weighted = (jnp.exp(cume - last) * x_ref[...].astype(F32)).astype(BF)
    state = lax.dot_general(
        write_ref[...], weighted, (((0,), (0,)), ((), ())), preferred_element_type=F32
    ).astype(BF)
    size = state.shape[0]
    high, low = split(jnp.exp(-last), 2)
    row = iota((PAD, cols), 0)
    tail = jnp.where(row == 0, high.astype(F32), jnp.where(row == 1, low.astype(F32), 0.0)).astype(BF)
    for q in range(n):
        pieces[q, 0:size, :] = state[:, q * piece : (q + 1) * piece]
        pieces[q, size : size + PAD, :] = tail[:, q * piece : (q + 1) * piece]
    for k in range(n):
        outs[k][...] = pieces[lax.rem(c + k, n)]


def prefix_kernel(n, scal, *refs):
    ins, outs, got, made = refs[:n], refs[n : 2 * n], refs[2 * n], refs[2 * n + 1]
    c = scal[0]
    size = outs[0].shape[0]
    for k in range(n):
        got[lax.rem(c + n - k, n)] = ins[k][...]
    total = jnp.zeros(outs[0].shape, F32)
    for j in range(n):
        made[j] = total.astype(BF)
        if j < n - 1:
            keep = got[j, size : size + PAD, :].astype(F32)
            keep = keep[0:1, :] + keep[1:2, :]
            total = total * keep + got[j, 0:size, :].astype(F32)
    for k in range(n):
        outs[k][...] = made[lax.rem(c + k, n)]


def within_kernel(count, width, x_ref, cume_ref, cumt_ref, write_ref, read_ref, skip_ref, out_ref, inter):
    rows = x_ref.shape[0]
    half = rows // 2
    step = pl.program_id(0)

    @pl.when(step == 0)
    def _():
        inter[...] = lax.dot_general(
            read_ref[...], write_ref[...], (((1,), (1,)), ((), ())), preferred_element_type=F32
        )

    causal = iota((half, half), 0) >= iota((half, half), 1)
    for j in range(count):
        lanes = slice(j * width, (j + 1) * width)
        x = x_ref[:, lanes]
        col = cume_ref[:, j * width : j * width + 1]
        line = cumt_ref[pl.ds(step * count + j, 1), :]
        top, bottom = col[0:half], col[half:rows]
        left, right = line[:, 0:half], line[:, half:rows]
        m00 = jnp.exp(jnp.where(causal, left - top, 0.0))
        m00 = jnp.where(causal, m00 * inter[0:half, 0:half], 0.0).astype(BF)
        m10 = (jnp.exp(left - bottom) * inter[half:rows, 0:half]).astype(BF)
        m11 = jnp.exp(jnp.where(causal, right - bottom, 0.0))
        m11 = jnp.where(causal, m11 * inter[half:rows, half:rows], 0.0).astype(BF)
        skip = skip_ref[:, lanes]
        xf = x.astype(F32)
        out_ref[0:half, lanes] = dot(m00, x[0:half]) + skip * xf[0:half]
        out_ref[half:rows, lanes] = (
            dot(m10, x[0:half]) + dot(m11, x[half:rows]) + skip * xf[half:rows]
        )


def gate_kernel(n, base, per, scal, base_ref, cume_ref, gate_ref, gain_ref, read_ref, *refs):
    ins, out_ref, prior = refs[:n], refs[n], refs[n + 1]
    c = scal[0]
    for k in range(n):
        prior[lax.rem(c + n - k, n)] = ins[k][...]
    reads = read_ref[...]
    carried = [dot(reads, prior[base + q]) for q in range(per)]
    carried = carried[0] if per == 1 else jnp.concatenate(carried, axis=1)
    mixed = base_ref[...] + carried * jnp.exp(-cume_ref[...])
    gate = gate_ref[...].astype(F32)
    gated = mixed * (gate / (1.0 + jnp.exp(-gate)))
    mean = jnp.mean(gated * gated, axis=1, keepdims=True)
    out_ref[...] = (gated * lax.rsqrt(mean + EPS) * gain_ref[...]).astype(BF)


def project_kernel(call, options, groups, grp, fold, parts, sel, scal, *refs):
    cands = refs[: options * groups]
    refs = refs[options * groups :]
    w_ref, refs = refs[0], refs[1:]
    if fold:
        add_ref, refs = refs[0], refs[1:]
    if parts == 2:
        keep_ref, send_ref, a, sem = refs
    else:
        keep_ref, a, sem = refs

    @pl.when(pl.program_id(0) == 0)
    def _():
        for o in range(options):

            @pl.when(sel[call] == o)
            def _():
                for g in range(groups):
                    pltpu.make_async_copy(cands[o * groups + g], a.at[g], sem.at[g]).start()

        for g in range(groups):
            pltpu.make_async_copy(cands[g], a.at[g], sem.at[g]).wait()

    total = sum(dot(a[g], w_ref[g * grp : (g + 1) * grp, :]) for g in range(groups))
    if fold:
        total = total + add_ref[...].astype(F32)
    total = total.astype(BF)
    if parts == 2:
        half = total.shape[0] // 2
        first = scal[2] == 0
        keep_ref[...] = jnp.where(first, total[:half], total[half:])
        send_ref[...] = jnp.where(first, total[half:], total[:half])
    else:
        keep_ref[...] = total


def project(call, sel, scal, cands, weight, add, parts):
    options, groups = len(cands), len(cands[0])
    rows, grp = cands[0][0].shape
    feats = weight.shape[1]
    tile = min(feats, 256)
    specs = [ANY] * (options * groups)
    specs.append(pl.BlockSpec((weight.shape[0], tile), lambda j, *_: (0, j)))
    args = [a for cand in cands for a in cand] + [weight]
    if add is not None:
        specs.append(pl.BlockSpec((rows, tile), lambda j, *_: (0, j)))
        args.append(add)
    out_rows = rows // parts
    out_spec = pl.BlockSpec((out_rows, tile), lambda j, *_: (0, j))
    return pl.pallas_call(
        functools.partial(project_kernel, call, options, groups, grp, add is not None, parts),
        grid_spec=pltpu.PrefetchScalarGridSpec(
            num_scalar_prefetch=2,
            grid=(feats // tile,),
            in_specs=specs,
            out_specs=[out_spec] * parts,
            scratch_shapes=[pltpu.VMEM((groups, rows, grp), BF), pltpu.SemaphoreType.DMA((groups,))],
        ),
        out_shape=[sds((out_rows, feats))] * parts,
        name="project",
    )(sel, scal, *args)


def route_kernel(wave, ids_ref, fixed_ref, placed_ref, table_ref):
    rows, named = ids_ref.shape
    ids, fixed = ids_ref[...], fixed_ref[...]
    lane = iota((rows, wave), 1)
    chosen = jnp.zeros((rows, wave), jnp.int32)
    weight = jnp.zeros((rows, wave), jnp.int32)
    for k in range(named):
        match = ids[:, k : k + 1] == lane
        chosen = jnp.where(match, 1, chosen)
        weight = weight + jnp.where(match, fixed[:, k : k + 1], 0)
    chosen = chosen.astype(F32)
    lower = (iota((rows, rows), 0) >= iota((rows, rows), 1)).astype(F32).astype(BF)
    slot = dot(lower, chosen.astype(BF)) - 1.0
    slots = wave * CAP
    spread = (iota((wave, slots), 1) // CAP == iota((wave, slots), 0)).astype(F32).astype(BF)
    slot = dot(jnp.where(chosen > 0.5, slot, -1.0).astype(BF), spread)
    route = (weight.astype(F32) / 65536.0).astype(BF)
    placed = slot == (iota((rows, slots), 1) % CAP).astype(F32)
    table_ref[...] = jnp.where(placed, dot(route, spread), 0.0).astype(BF)
    placed_ref[...] = jnp.where(placed, 1.0, 0.0).T.astype(BF)


def pick_half(core, value):
    half = value.shape[1] // 2
    first = core == 0
    mine = jnp.where(first, value[:, :half], value[:, half:])
    other = jnp.where(first, value[:, half:], value[:, :half])
    return mine, other


def squares_block(value):
    high, low = split(value, 2)
    lane = iota((value.shape[0], SQL), 1)
    high, low = high.astype(F32), low.astype(F32)
    return jnp.where(lane == 0, high, jnp.where(lane == 1, low, 0.0)).astype(BF)


def latent_kernel(where_to, scal, resin_ref, gain_ref, down_ref, placed_ref, *refs):
    count = len(where_to)
    ins = refs[:count]
    res_ref, keep_ref, send_ref = refs[count:]
    done = set()
    for (r0, c0), ref in zip(where_to, ins):
        at = (slice(r0, r0 + ref.shape[0]), slice(c0, c0 + ref.shape[1]))
        value = ref[...].astype(F32)
        if (r0, c0) in done:
            res_ref[at] += value
        else:
            res_ref[at] = value + resin_ref[at].astype(F32)
            done.add((r0, c0))
    residual = res_ref[...]
    placed = placed_ref[...]
    scaled = dot(placed, (residual * gain_ref[...]).astype(BF)).astype(BF)
    part = dot(scaled, down_ref[...])
    squares = jnp.sum(residual * residual, axis=1, keepdims=True)
    squares = dot(placed, squares_block(squares)).astype(BF)
    mine, other = pick_half(scal[1], part)
    half = mine.shape[1]
    keep_ref[:, :half] = mine
    keep_ref[:, half:] = squares.astype(F32)
    send_ref[:, :half] = other.astype(BF)
    send_ref[:, half:] = squares


def dispatch_kernel(n, scal, keep_ref, recv_ref, *refs):
    outs, total = refs[:n], refs[n]
    c = scal[0]
    half = keep_ref.shape[1] - SQL
    rows = outs[0].shape[0]
    total[:, :half] = (keep_ref[:, :half] + recv_ref[:, :half].astype(F32)).astype(BF)
    squares = keep_ref[:, half:] + recv_ref[:, half:].astype(F32)
    total[:, half:] = squares_block(squares[:, 0:1] + squares[:, 1:2])
    for k in range(n):
        start = pl.multiple_of(lax.rem(c + k, n) * rows, rows)
        outs[k][...] = total[pl.ds(start, rows), :]


def gather_kernel(n, nx, width, *refs):
    ins, out_ref = refs[: n * nx], refs[n * nx]
    rows = ins[0].shape[0]
    half = out_ref.shape[1]
    for k in range(n):
        total = sum(ins[k * nx + d][...].astype(F32) for d in range(nx))
        square = total[:, half : half + 1] + total[:, half + 1 : half + 2]
        inv = lax.rsqrt(square / width + EPS)
        out_ref[k * rows : (k + 1) * rows, :] = (total[:, :half] * inv).astype(BF)


def expert_kernel(n, scal, mine_ref, other_ref, up_ref, down_ref, keep_ref, send_ref):
    e = pl.program_id(0)
    stride = mine_ref.shape[0] // n
    half = mine_ref.shape[1]

    def rows_of(ref):
        parts = [ref[pl.ds(pl.multiple_of(k * stride + e * CAP, CAP), CAP), :] for k in range(n)]
        return jnp.concatenate(parts, axis=0)

    mine, other = rows_of(mine_ref), rows_of(other_ref)
    first = scal[1] == 0
    left = jnp.where(first, mine, other)
    right = jnp.where(first, other, mine)
    hidden = dot(left, up_ref[0, :half, :]) + dot(right, up_ref[0, half:, :])
    hidden = jnp.maximum(hidden, 0.0)
    out = dot((hidden * hidden).astype(BF), down_ref[0])
    mine, other = pick_half(scal[1], out)
    keep_ref[0] = mine
    send_ref[0] = other.astype(BF)


def give_back_kernel(n, keep_ref, recv_ref, *outs):
    for e in range(keep_ref.shape[0]):
        total = (keep_ref[e] + recv_ref[e].astype(F32)).astype(BF)
        for k in range(n):
            outs[k][e * CAP : (e + 1) * CAP, :] = total[k * CAP : (k + 1) * CAP, :]


def returned_kernel(n, nx, scal, *refs):
    ins, out_ref = refs[: n * nx], refs[n * nx]
    c = scal[0]
    rows = ins[0].shape[0]
    for k in range(n):
        total = sum(ins[k * nx + d][...].astype(F32) for d in range(nx))
        start = pl.multiple_of(lax.rem(c + k, n) * rows, rows)
        out_ref[pl.ds(start, rows), :] = total.astype(BF)


def combine_kernel(scal, mine_ref, other_ref, table_ref, res_ref, up_ref, out_ref):
    first = scal[1] == 0
    mine, other = mine_ref[...], other_ref[...]
    table = table_ref[...]
    half = mine.shape[1]
    left = dot(table, jnp.where(first, mine, other)).astype(BF)
    right = dot(table, jnp.where(first, other, mine)).astype(BF)
    moe = dot(left, up_ref[:half, :]) + dot(right, up_ref[half:, :])
    out_ref[...] = (res_ref[...] + moe).astype(BF)


def local(
    ssm_input,
    decay_log,
    state_write,
    state_read,
    skip_scale,
    gate_input,
    ssm_gain,
    out_weight,
    residual_in,
    moe_gain,
    down_latent,
    expert_up,
    expert_down,
    up_latent,
    expert_ids,
    combine_fixed,
):
    n, nh = lax.axis_size("ctx"), lax.axis_size("heads")
    nx = nh // 2
    c, h = lax.axis_index("ctx"), lax.axis_index("heads")
    both = ("ctx", "heads")
    rows, cols = ssm_input.shape
    heads = decay_log.shape[1]
    width = cols // heads
    size = state_write.shape[1]
    groups = cols // GRP
    piece = cols // n
    feats = residual_in.shape[1]
    slots = expert_up.shape[0] * n * CAP
    per_owner = expert_up.shape[0] * CAP
    lat = down_latent.shape[1]
    half = lat // 2
    scal = jnp.stack([c, h % 2, (h // 2) % 2]).astype(jnp.int32)

    def turn(k):
        return [(i, (i + k) % n) for i in range(n)]

    outs = pl.pallas_call(
        functools.partial(state_kernel, n, heads, width),
        in_specs=[SM, VM, VM, VM],
        out_specs=[VM] * (n + 2),
        out_shape=[sds((rows, cols), F32), sds((heads, rows), F32)] + [sds((size + PAD, piece))] * n,
        scratch_shapes=[pltpu.VMEM((n, size + PAD, piece), BF)],
        name="state",
    )(scal, ssm_input, decay_log, state_write)
    cume, cumt, sends = outs[0], outs[1], outs[2:]
    got = [sends[0]] + [lax.ppermute(sends[k], "ctx", turn(k)) for k in range(1, n)]
    prior = pl.pallas_call(
        functools.partial(prefix_kernel, n),
        in_specs=[SM] + [VM] * n,
        out_specs=[VM] * n,
        out_shape=[sds((size, piece))] * n,
        scratch_shapes=[pltpu.VMEM((n, size + PAD, piece), BF), pltpu.VMEM((n, size, piece), BF)],
        name="prefix",
    )(scal, *got)
    prior = [prior[0]] + [lax.ppermute(prior[k], "ctx", turn(k)) for k in range(1, n)]
    count = min(heads, 8)
    block = count * width
    base = pl.pallas_call(
        functools.partial(within_kernel, count, width),
        grid=(heads // count,),
        in_specs=[
            pl.BlockSpec((rows, block), lambda i: (0, i)),
            pl.BlockSpec((rows, block), lambda i: (0, i)),
            pl.BlockSpec((heads, rows), lambda i: (0, 0)),
            pl.BlockSpec((rows, size), lambda i: (0, 0)),
            pl.BlockSpec((rows, size), lambda i: (0, 0)),
            pl.BlockSpec((1, block), lambda i: (0, i)),
        ],
        out_specs=pl.BlockSpec((rows, block), lambda i: (0, i)),
        out_shape=sds((rows, cols), F32),
        scratch_shapes=[pltpu.VMEM((rows, rows), F32)],
        name="within",
    )(ssm_input, cume, cumt, state_write, state_read, jnp.repeat(skip_scale, width)[None, :])
    placed, table = pl.pallas_call(
        functools.partial(route_kernel, slots // CAP),
        in_specs=[VM] * 2,
        out_specs=[VM] * 2,
        out_shape=[sds((slots, rows)), sds((rows, slots))],
        name="route",
    )(expert_ids, combine_fixed)
    per = GRP // piece
    normed = []
    for g in range(groups):
        at = pl.BlockSpec((rows, GRP), lambda i, g=g: (0, g))
        line = pl.BlockSpec((1, GRP), lambda i, g=g: (0, g))
        full = pl.BlockSpec((rows, size), lambda i: (0, 0))
        small = pl.BlockSpec((size, piece), lambda i: (0, 0))
        normed.append(
            pl.pallas_call(
                functools.partial(gate_kernel, n, g * per, per),
                grid=(1,),
                in_specs=[SM, at, at, at, line, full] + [small] * n,
                out_specs=pl.BlockSpec((rows, GRP), lambda i: (0, 0)),
                out_shape=sds((rows, GRP)),
                scratch_shapes=[pltpu.VMEM((n, size, piece), BF)],
                name=f"gate{g}",
            )(scal, base, cume, gate_input, ssm_gain[None, :], state_read, *prior)
        )

    blocks = {("O", 0): normed}
    right = left = normed
    for s in range(1, n):
        right = [lax.ppermute(a, "ctx", [(i, i + 1) for i in range(s - 1, n - 1)]) for a in right]
        left = [lax.ppermute(a, "ctx", [(i, i - 1) for i in range(1, n - s + 1)]) for a in left]
        blocks["R", s], blocks["L", s] = right, left
    table_of = arrivals(n)
    calls, choose = [], [[] for _ in range(2 * n)]
    for p in range(n // 2):
        for sending in (True, False):
            keys = []
            for i in range(2 * n):
                cc, core = divmod(i, 2)
                key = table_of[cc][2 * p + (core ^ int(sending))][:2]
                if key not in keys:
                    keys.append(key)
                choose[i].append(keys.index(key))
            calls.append(keys)
    sel = lax.dynamic_index_in_dim(jnp.array(choose, jnp.int32), c * 2 + h % 2, 0, keepdims=False)
    ratio = n // nh
    feat_block = out_weight.shape[1]
    got, where_to = [], []
    for p in range(n // 2):
        (sent,) = project(2 * p, sel, scal, [blocks[k] for k in calls[2 * p]], out_weight, None, 1)
        recv = lax.ppermute(sent, "heads", [(i, i ^ 1) for i in range(nh)])
        parts = 2 if nx > 1 else 1
        outs = project(2 * p + 1, sel, scal, [blocks[k] for k in calls[2 * p + 1]], out_weight, recv, parts)
        held = outs[0]
        if nx > 1:
            held = held + lax.ppermute(outs[1], "heads", [(i, i ^ 2) for i in range(nh)])
        bit = 4
        while bit < nh:
            length = held.shape[0] // 2
            here = (h // bit) % 2
            mine = lax.dynamic_slice_in_dim(held, here * length, length, 0)
            other = lax.dynamic_slice_in_dim(held, (1 - here) * length, length, 0)
            held = mine + lax.ppermute(other, "heads", [(i, i ^ bit) for i in range(nh)])
            bit *= 2
        length = held.shape[0]
        for xi in range(nx):
            at, bit, span = 0, 1, rows
            while bit < nx:
                span //= 2
                at += span * ((xi // bit) % 2)
                bit *= 2
            for rr in range(ratio):
                perm = []
                for cc in range(rr, n, ratio):
                    for core in range(2):
                        to = table_of[cc][2 * p + core][2]
                        perm.append((cc * nh + 2 * xi + core, to * nh + cc // ratio))
                got.append(lax.ppermute(held, both, perm))
                where_to.append((at, rr * feat_block))

    wide = half + SQL
    residual, keep, send = pl.pallas_call(
        functools.partial(latent_kernel, tuple(where_to)),
        in_specs=[SM] + [VM] * (4 + len(got)),
        out_specs=[VM] * 3,
        out_shape=[sds((rows, feats), F32), sds((slots, wide), F32), sds((slots, wide))],
        name="latent",
    )(scal, residual_in, moe_gain[None, :], down_latent, placed, *got)
    swap = [(i, i ^ 1) for i in range(nh)]
    recv = lax.ppermute(send, "heads", swap)
    sends = pl.pallas_call(
        functools.partial(dispatch_kernel, n),
        in_specs=[SM, VM, VM],
        out_specs=[VM] * n,
        out_shape=[sds((per_owner, wide))] * n,
        scratch_shapes=[pltpu.VMEM((slots, wide), BF)],
        name="dispatch",
    )(scal, keep, recv)

    def spread_out(arrays, sign):
        result = []
        for k in range(n):
            for d in range(nx):
                if k == 0 and d == 0:
                    result.append(arrays[0])
                    continue
                perm = []
                for cc in range(n):
                    for hh in range(nh):
                        to = ((cc + sign * k) % n) * nh + ((hh // 2 + d) % nx) * 2 + hh % 2
                        perm.append((cc * nh + hh, to))
                result.append(lax.ppermute(arrays[k], both, perm))
        return result

    mine = pl.pallas_call(
        functools.partial(gather_kernel, n, nx, float(feats * nh)),
        in_specs=[VM] * (n * nx),
        out_specs=VM,
        out_shape=sds((n * per_owner, half)),
        name="gather",
    )(*spread_out(sends, 1))
    other = lax.ppermute(mine, "heads", swap)
    owned, hidden = expert_up.shape[0], expert_up.shape[2]
    whole = pl.BlockSpec((n * per_owner, half), lambda e: (0, 0))
    result = pl.BlockSpec((1, n * CAP, half), lambda e: (e, 0, 0))
    keep, send = pl.pallas_call(
        functools.partial(expert_kernel, n),
        grid=(owned,),
        in_specs=[
            SM,
            whole,
            whole,
            pl.BlockSpec((1, lat, hidden), lambda e: (e, 0, 0)),
            pl.BlockSpec((1, hidden, lat), lambda e: (e, 0, 0)),
        ],
        out_specs=[result, result],
        out_shape=[sds((owned, n * CAP, half), F32), sds((owned, n * CAP, half))],
        name="expert",
    )(scal, mine, other, expert_up, expert_down)
    recv = lax.ppermute(send, "heads", swap)
    sends = pl.pallas_call(
        functools.partial(give_back_kernel, n),
        in_specs=[VM, VM],
        out_specs=[VM] * n,
        out_shape=[sds((per_owner, half))] * n,
        name="give_back",
    )(keep, recv)
    mine = pl.pallas_call(
        functools.partial(returned_kernel, n, nx),
        in_specs=[SM] + [VM] * (n * nx),
        out_specs=VM,
        out_shape=sds((slots, half)),
        name="returned",
    )(scal, *spread_out(sends, -1))
    other = lax.ppermute(mine, "heads", swap)
    return pl.pallas_call(
        combine_kernel,
        in_specs=[SM] + [VM] * 5,
        out_specs=VM,
        out_shape=sds((rows, feats)),
        name="combine",
    )(scal, mine, other, table, residual, up_latent)


def solution(mesh):
    placed = (
        P(("groups", "ctx"), "heads"),
        P(("groups", "ctx"), "heads"),
        P(("groups", "ctx"), None),
        P(("groups", "ctx"), None),
        P("heads"),
        P(("groups", "ctx"), "heads"),
        P("heads"),
        P("heads", "ctx"),
        P(("groups", "ctx"), "heads"),
        P("heads"),
        P("heads", None),
        P("ctx", None, "heads"),
        P("ctx", "heads", None),
        P(None, "heads"),
        P(("groups", "ctx"), None),
        P(("groups", "ctx"), None),
    )
    return jax.shard_map(
        local, mesh=mesh, in_specs=placed, out_specs=P(("groups", "ctx"), "heads"), check_vma=False
    )
```

```python
import functools

import jax
import jax.numpy as jnp
from jax import lax
from jax.experimental import pallas as pl
from jax.experimental.pallas import tpu as pltpu
from jax.sharding import PartitionSpec as P


GRP = 1024
CAP = 16
EPS = 1e-05
PAD = 16
SQL = 128
LANES = 128
BF = jnp.bfloat16
F32 = jnp.float32

VM = pl.BlockSpec(memory_space=pltpu.VMEM)
LIMIT = 14 * 2**20


def sds(shape, dtype=BF):
    return pltpu.VMEM(shape, dtype)


def call(body, args, outs, scratch=()):
    args = [pltpu.with_memory_space_constraint(a, pltpu.VMEM) for a in args]
    return pl.pallas_call(
        body,
        in_specs=[VM] * len(args),
        out_specs=[VM] * len(outs),
        out_shape=outs,
        scratch_shapes=scratch,
        compiler_params=pltpu.CompilerParams(vmem_limit_bytes=LIMIT),
    )(*args)


def pick(table, index):
    value = jnp.int32(table[0])
    for i, entry in enumerate(table[1:], 1):
        if entry != table[0]:
            value = jnp.where(index == i, jnp.int32(entry), value)
    return value


def dot(a, b):
    return jnp.dot(a, b, preferred_element_type=F32)


def split(v, terms):
    out = []
    for _ in range(terms):
        part = v.astype(BF)
        out.append(part)
        v = v - part.astype(F32)
    return out


def iota(shape, dim):
    return lax.broadcasted_iota(jnp.int32, shape, dim)


def plan_of(rows, shares):
    units = rows // shares // LANES
    sizes = (1, 2, 1, 2, 2)
    if units % sum(sizes) == 0:
        return tuple(size * units // sum(sizes) * LANES for size in sizes)
    return (LANES,) * units


def tasks(n):
    table = []
    for c in range(n):
        row = [("O", 0, c)]
        for s in range(1, n - 1):
            if c - s >= 0:
                row.append(("R", s, c - s))
            if c + s < n:
                row.append(("L", s, c + s))
        if len(row) < n:
            row.insert(n - 2, None)
        table.append(row)
    return table


def state_kernel(n, heads, width, x_ref, decay_ref, write_ref, scale_ref, cume_ref, cumt_ref, skip_ref, *rest):
    outs, pieces = rest[:n], rest[n]
    rows = x_ref.shape[0]
    cols = heads * width
    piece = cols // n
    c = lax.axis_index("ctx")
    upper = (iota((rows, rows), 0) <= iota((rows, rows), 1)).astype(F32).astype(BF)
    cumt = sum(dot(part, upper) for part in split(decay_ref[...], 3))
    cumt_ref[...] = cumt
    cum = cumt.T
    spread = (iota((heads, cols), 1) // width == iota((heads, cols), 0)).astype(F32).astype(BF)
    cume = sum(dot(part, spread) for part in split(cum, 3))
    cume_ref[...] = cume
    skip_ref[...] = sum(dot(part, spread) for part in split(scale_ref[...], 3))
    last = cume[rows - 1 : rows, :]
    weighted = (jnp.exp(cume - last) * x_ref[...].astype(F32)).astype(BF)
    state = lax.dot_general(
        write_ref[...], weighted, (((0,), (0,)), ((), ())), preferred_element_type=F32
    ).astype(BF)
    size = state.shape[0]
    high, low = split(jnp.exp(-last), 2)
    row = iota((PAD, cols), 0)
    tail = jnp.where(row == 0, high.astype(F32), jnp.where(row == 1, low.astype(F32), 0.0)).astype(BF)
    for q in range(n):
        pieces[q, 0:size, :] = state[:, q * piece : (q + 1) * piece]
        pieces[q, size : size + PAD, :] = tail[:, q * piece : (q + 1) * piece]
    for k in range(n):
        outs[k][...] = pieces[c ^ k]


def prefix_kernel(n, *refs):
    ins, outs, got, made = refs[:n], refs[n : 2 * n], refs[2 * n], refs[2 * n + 1]
    c = lax.axis_index("ctx")
    size = outs[0].shape[0]
    for k in range(n):
        got[c ^ k] = ins[k][...]
    total = jnp.zeros(outs[0].shape, F32)
    for j in range(n):
        made[j] = total.astype(BF)
        if j < n - 1:
            keep = got[j, size : size + PAD, :].astype(F32)
            keep = keep[0:1, :] + keep[1:2, :]
            total = total * keep + got[j, 0:size, :].astype(F32)
    for k in range(n):
        outs[k][...] = made[c ^ k]


def within_kernel(first, steps, count, width, x_ref, cume_ref, cumt_ref, write_ref, read_ref, skip_ref, out_ref):
    rows = x_ref.shape[0]
    half = rows // 2
    inter = lax.dot_general(
        read_ref[...], write_ref[...], (((1,), (1,)), ((), ())), preferred_element_type=F32
    )
    causal = iota((half, half), 0) >= iota((half, half), 1)
    block = count * width

    def step(i, carry):
        start = pl.multiple_of((first + i) * block, block)
        x_all = x_ref[:, pl.ds(start, block)]
        cume = cume_ref[:, pl.ds(start, block)]
        skip_all = skip_ref[:, pl.ds(start, block)]
        results = []
        for j in range(count):
            lanes = slice(j * width, (j + 1) * width)
            x = x_all[:, lanes]
            col = cume[:, j * width : j * width + 1]
            line = cumt_ref[pl.ds((first + i) * count + j, 1), :]
            top, bottom = col[0:half], col[half:rows]
            left, right = line[:, 0:half], line[:, half:rows]
            m00 = jnp.exp(jnp.where(causal, left - top, 0.0))
            m00 = jnp.where(causal, m00 * inter[0:half, 0:half], 0.0).astype(BF)
            m10 = (jnp.exp(left - bottom) * inter[half:rows, 0:half]).astype(BF)
            m11 = jnp.exp(jnp.where(causal, right - bottom, 0.0))
            m11 = jnp.where(causal, m11 * inter[half:rows, half:rows], 0.0).astype(BF)
            upper = dot(m00, x[0:half])
            lower = dot(m10, x[0:half]) + dot(m11, x[half:rows])
            results.append(jnp.concatenate([upper, lower], axis=0))
        result = results[0] if count == 1 else jnp.concatenate(results, axis=1)
        at = pl.ds(pl.multiple_of(i * block, block), block)
        out_ref[:, at] = result + skip_all * x_all.astype(F32)
        return carry

    lax.fori_loop(0, steps, step, 0)


def gate_kernel(n, base, per, base_ref, cume_ref, gate_ref, gain_ref, read_ref, *refs):
    ins, out_ref, prior = refs[:n], refs[n], refs[n + 1]
    c = lax.axis_index("ctx")
    at = slice(base * (GRP // per), (base + per) * (GRP // per))
    for k in range(n):
        prior[c ^ k] = ins[k][...]
    reads = read_ref[...]
    carried = [dot(reads, prior[base + q]) for q in range(per)]
    carried = carried[0] if per == 1 else jnp.concatenate(carried, axis=1)
    mixed = base_ref[...] + carried * jnp.exp(-cume_ref[:, at])
    gate = gate_ref[:, at].astype(F32)
    gated = mixed * (gate / (1.0 + jnp.exp(-gate)))
    mean = jnp.mean(gated * gated, axis=1, keepdims=True)
    out_ref[...] = (gated * lax.rsqrt(mean + EPS) * gain_ref[:, at]).astype(BF)


def load_rows(choice, index, options, groups, cands, a):
    grp = a.shape[1] // groups
    sel = pick(choice, index)
    for o in range(options):

        def copy(o=o):
            for g in range(groups):
                a[:, g * grp : (g + 1) * grp] = cands[o * groups + g][...]

        if len(set(choice)) == 1:
            if o == choice[0]:
                copy()
        else:
            pl.when(sel == o)(copy)


def store_parts(total, outs):
    total = total.astype(BF)
    if len(outs) == 2:
        half = total.shape[0] // 2
        first = lax.rem(lax.axis_index("heads") // 2, 2) == 0
        outs[0][...] = jnp.where(first, total[:half], total[half:])
        outs[1][...] = jnp.where(first, total[half:], total[:half])
    else:
        outs[0][...] = total


def project_kernel(choice, options, groups, fold, parts, *refs):
    cands, refs = refs[: options * groups], refs[options * groups :]
    w_ref, refs = refs[0], refs[1:]
    if fold:
        add_ref, refs = refs[0], refs[1:]
    outs, a = refs[:parts], refs[parts]
    place = lax.axis_index("ctx") * 2 + lax.rem(lax.axis_index("heads"), 2)
    load_rows(choice, place, options, groups, cands, a)
    total = dot(a[...], w_ref[...])
    if fold:
        total = total + add_ref[...].astype(F32)
    store_parts(total, outs)


def final_kernel(choice, options, groups, far_core, shares, chunks, fold, parts, *refs):
    cands, refs = refs[: options * groups], refs[options * groups :]
    w_ref, refs = refs[0], refs[1:]
    far, refs = refs[: shares * chunks], refs[shares * chunks :]
    if fold:
        add_ref, refs = refs[0], refs[1:]
    outs, a, acc = refs[:parts], refs[parts], refs[parts + 1]
    place = lax.axis_index("ctx") * 2 + lax.rem(lax.axis_index("heads"), 2)
    load_rows(choice, place, options, groups, cands, a)
    core = lax.rem(lax.axis_index("heads"), 2)
    plan = [far[j].shape[0] for j in range(chunks)]

    @pl.when(core == far_core)
    def _():
        total = None
        for k in range(shares):
            share = lax.axis_index("groups") ^ k
            for j in range(chunks):
                start = pl.multiple_of(share * sum(plan) + sum(plan[:j]), LANES)
                part = dot(a[:, pl.ds(start, plan[j])], far[k * chunks + j][...])
                total = part if total is None else total + part
        acc[...] = total

    @pl.when(core != far_core)
    def _():
        acc[...] = dot(a[...], w_ref[...])

    total = acc[...]
    if fold:
        total = total + add_ref[...].astype(F32)
    store_parts(total, outs)


def project(choice, cands, weight, add, parts):
    options, groups = len(cands), len(cands[0])
    rows, grp = cands[0][0].shape
    args = [a for cand in cands for a in cand] + [weight]
    if add is not None:
        args.append(add)
    return call(
        functools.partial(project_kernel, choice, options, groups, add is not None, parts),
        args,
        [sds((rows // parts, weight.shape[1]))] * parts,
        [pltpu.VMEM((rows, groups * grp), BF)],
    )


def project_final(choice, cands, weight, far, far_core, add, parts):
    options, groups = len(cands), len(cands[0])
    rows, grp = cands[0][0].shape
    args = [a for cand in cands for a in cand] + [weight] + [a for share in far for a in share]
    if add is not None:
        args.append(add)
    return call(
        functools.partial(
            final_kernel, choice, options, groups, far_core, len(far), len(far[0]), add is not None, parts
        ),
        args,
        [sds((rows // parts, weight.shape[1]))] * parts,
        [pltpu.VMEM((rows, groups * grp), BF), pltpu.VMEM((rows, weight.shape[1]), F32)],
    )


def fold_kernel(own_ref, add_ref, *outs):
    store_parts(own_ref[...].astype(F32) + add_ref[...].astype(F32), outs)


def fold(own, add, parts):
    shape = (own.shape[0] // parts, own.shape[1])
    return call(fold_kernel, [own, add], [sds(shape)] * parts)


def cut_kernel(plan, picks, w_ref, *refs):
    outs, sem = refs[:-1], refs[-1]
    share = lax.axis_index("groups") * sum(plan)
    copies = []
    for i, (j, out) in enumerate(zip(picks, outs)):
        start = pl.multiple_of(share + sum(plan[:j]), LANES)
        copies.append(
            pltpu.make_async_copy(w_ref.at[pl.ds(start, plan[j]), :], out, sem.at[i])
        )
    for copy in copies:
        copy.start()
    for copy in copies:
        copy.wait()


def cut(weight, space, plan, picks):
    return pl.pallas_call(
        functools.partial(cut_kernel, plan, picks),
        in_specs=[pl.BlockSpec(memory_space=space)],
        out_specs=[VM] * len(picks),
        out_shape=[sds((plan[j], weight.shape[1])) for j in picks],
        scratch_shapes=[pltpu.SemaphoreType.DMA((len(picks),))],
        compiler_params=pltpu.CompilerParams(vmem_limit_bytes=LIMIT),
        name="cut",
    )(pltpu.with_memory_space_constraint(weight, space))


def route_kernel(owners, owned, ids_ref, fixed_ref, placed_ref, table_ref):
    named, rows = ids_ref.shape
    wave = owners * owned
    ids, fixed = ids_ref[...], fixed_ref[...]
    line = iota((wave, rows), 0)
    chosen = jnp.zeros((wave, rows), jnp.int32)
    weight = jnp.zeros((wave, rows), jnp.int32)
    for k in range(named):
        match = ids[k : k + 1, :] == line
        chosen = jnp.where(match, 1, chosen)
        weight = weight + jnp.where(match, fixed[k : k + 1, :], 0)
    chosen = chosen.astype(F32)
    upper = (iota((rows, rows), 0) <= iota((rows, rows), 1)).astype(F32).astype(BF)
    slot = dot(chosen.astype(BF), upper) - 1.0
    slot = jnp.where(chosen > 0.5, slot, -1.0).astype(BF)
    route = (weight.astype(F32) / 65536.0).astype(BF)
    slots = wave * CAP
    per = owned // 2
    s = iota((slots, wave), 0) // CAP
    expert = (s // per % owners) * owned + s // (per * owners) * per + s % per
    spread = (expert == iota((slots, wave), 1)).astype(F32).astype(BF)
    placed = dot(spread, slot) == (iota((slots, rows), 0) % CAP).astype(F32)
    table_ref[...] = jnp.where(placed, dot(spread, route), 0.0).T.astype(BF)
    placed_ref[...] = jnp.where(placed, 1.0, 0.0).astype(BF)


def by_core(value):
    half = value.shape[0] // 2
    first = lax.rem(lax.axis_index("heads"), 2) == 0
    mine = jnp.where(first, value[:half], value[half:])
    other = jnp.where(first, value[half:], value[:half])
    return mine, other


def squares_block(value):
    high, low = split(value, 2)
    lane = iota((value.shape[0], SQL), 1)
    high, low = high.astype(F32), low.astype(F32)
    return jnp.where(lane == 0, high, jnp.where(lane == 1, low, 0.0)).astype(BF)


def latent_kernel(where_to, resin_ref, gain_ref, down_ref, placed_ref, *refs):
    count = len(where_to)
    ins = refs[:count]
    res_ref, same_ref, other_ref = refs[count:]
    done = set()
    for (r0, c0), ref in zip(where_to, ins):
        at = (slice(r0, r0 + ref.shape[0]), slice(c0, c0 + ref.shape[1]))
        value = ref[...].astype(F32)
        if (r0, c0) in done:
            res_ref[at] += value
        else:
            res_ref[at] = value + resin_ref[at].astype(F32)
            done.add((r0, c0))
    residual = res_ref[...]
    placed = placed_ref[...]
    scaled = dot(placed, (residual * gain_ref[...]).astype(BF)).astype(BF)
    squares = jnp.sum(residual * residual, axis=1, keepdims=True)
    squares = dot(placed, squares_block(squares)).astype(BF)
    lat = down_ref.shape[1]
    mine, other = by_core(dot(scaled, down_ref[...]))
    same_ref[:, :lat] = mine.astype(BF)
    other_ref[:, :lat] = other.astype(BF)
    mine, other = by_core(squares)
    same_ref[:, lat:] = mine
    other_ref[:, lat:] = other


def add_up(ins, total):
    lat = total.shape[1] - SQL
    total[:, :lat] = sum(ref[:, :lat].astype(F32) for ref in ins).astype(BF)
    squares = sum(ref[:, lat:].astype(F32) for ref in ins)
    total[:, lat:] = squares_block(squares[:, 0:1] + squares[:, 1:2])


def merge_kernel(own_ref, recv_ref, out_ref):
    add_up((own_ref, recv_ref), out_ref)


def dispatch_kernel(n, count, *refs):
    ins, outs, total = refs[:count], refs[count : count + n], refs[count + n]
    c = lax.axis_index("ctx")
    rows = outs[0].shape[0]
    add_up(ins, total)
    for k in range(n):
        start = pl.multiple_of((c ^ k) * rows, rows)
        outs[k][...] = total[pl.ds(start, rows), :]


def expert_kernel(n, per, features, *refs):
    ins = refs[:n]
    up_ref, down_ref, up_other_ref, down_other_ref = refs[n : n + 4]
    outs = refs[n + 4 :]
    lat = outs[0].shape[1]
    contract = (((1,), (1,)), ((), ()))
    for j in range(per):
        rows = jnp.concatenate([ref[j * CAP : (j + 1) * CAP, :] for ref in ins], axis=0)
        square = rows[:, lat : lat + 1].astype(F32) + rows[:, lat + 1 : lat + 2].astype(F32)
        rows = (rows[:, :lat].astype(F32) * lax.rsqrt(square / features + EPS)).astype(BF)
        result = None
        for up, down in (
            (up_ref[j], down_ref[j]),
            (up_other_ref[j], down_other_ref[j]),
        ):
            hidden = lax.dot_general(rows, up, contract, preferred_element_type=F32)
            hidden = jnp.maximum(hidden, 0.0)
            part = dot((hidden * hidden).astype(BF), down)
            result = part if result is None else result + part
        result = result.astype(BF)
        for k in range(n):
            outs[k][j * CAP : (j + 1) * CAP, :] = result[k * CAP : (k + 1) * CAP, :]


def share_kernel(per, *refs):
    count = (len(refs) - 1) // 3
    ins, outs, sem = refs[:count], refs[count : 3 * count], refs[3 * count]
    core = lax.rem(lax.axis_index("heads"), 2)
    copies = []
    for i, ref in enumerate(ins):
        for k, start in enumerate((core * per, (1 - core) * per)):
            copies.append(
                pltpu.make_async_copy(
                    ref.at[pl.ds(start, per)], outs[i + k * count], sem.at[i + k * count]
                )
            )
    for copy in copies:
        copy.start()
    for copy in copies:
        copy.wait()


def share_experts(per, *arrays):
    outs = pl.pallas_call(
        functools.partial(share_kernel, per),
        in_specs=[pl.BlockSpec(memory_space=pl.ANY)] * len(arrays),
        out_specs=[VM] * (2 * len(arrays)),
        out_shape=[sds((per, *a.shape[1:])) for a in arrays] * 2,
        scratch_shapes=[pltpu.SemaphoreType.DMA((2 * len(arrays),))],
        compiler_params=pltpu.CompilerParams(vmem_limit_bytes=LIMIT),
        name="share",
    )(*arrays)
    return outs[: len(arrays)], outs[len(arrays) :]


def returned_kernel(n, *refs):
    ins, out_ref = refs[:n], refs[n]
    c = lax.axis_index("ctx")
    rows = ins[0].shape[0]
    for k in range(n):
        out_ref[pl.ds(pl.multiple_of((c ^ k) * rows, rows), rows), :] = ins[k][...]


def sum_kernel(*refs):
    refs[-1][...] = sum(ref[...].astype(F32) for ref in refs[:-1]).astype(BF)


def combine_kernel(mine_ref, other_ref, table_ref, res_ref, up_ref, out_ref):
    mine, other = mine_ref[...], other_ref[...]
    first = lax.rem(lax.axis_index("heads"), 2) == 0
    table = table_ref[...]
    half = table.shape[1] // 2
    combined = dot(table[:, :half], jnp.where(first, mine, other))
    combined = combined + dot(table[:, half:], jnp.where(first, other, mine))
    out_ref[...] = (res_ref[...] + dot(combined.astype(BF), up_ref[...])).astype(BF)


def local(
    ssm_input,
    decay_log,
    state_write,
    state_read,
    skip_scale,
    gate_input,
    ssm_gain,
    out_weight,
    residual_in,
    moe_gain,
    down_latent,
    expert_up,
    expert_down,
    up_latent,
    expert_ids,
    combine_fixed,
):
    n, nh = lax.axis_size("ctx"), lax.axis_size("heads")
    nx, ny = nh // 2, lax.axis_size("groups")
    both = ("ctx", "heads")
    rows, cols = ssm_input.shape
    heads = decay_log.shape[1]
    width = cols // heads
    size = state_write.shape[1]
    groups = cols // GRP
    piece = cols // n
    feats = residual_in.shape[1]
    owned = expert_up.shape[0]
    per = owned // 2
    slots = owned * n * CAP
    lat = down_latent.shape[1]
    swap = [(i, i ^ 1) for i in range(nh)]

    def exchange(arrays, senders=range(n), receivers=range(n)):
        out = [arrays[0]]
        for k in range(1, n):
            perm = [(i, i ^ k) for i in senders if i ^ k in receivers]
            out.append(lax.ppermute(arrays[k], "ctx", perm))
        return out

    def across(a):
        out = [a]
        for k in range(1, nx):
            out.append(lax.ppermute(a, "heads", [(i, i ^ (2 * k)) for i in range(nh)]))
        return out

    plan = plan_of(out_weight.shape[0], ny)
    chunks = cut(out_weight, pltpu.HBM, plan, range(1))
    chunks = chunks + cut(out_weight, pl.ANY, plan, range(1, len(plan)))
    far = [[] for _ in range(ny)]
    for j, chunk in enumerate(chunks):
        far[0].append(lax.ppermute(chunk, "ctx", [(0, 1), (n - 1, n - 2)]))
        for k in range(1, ny):
            perm = []
            for y in range(ny):
                perm += [(y * n + c, (y ^ k) * n + c) for c in (1, n - 2)]
            far[k].append(lax.ppermute(far[0][j], ("groups", "ctx"), perm))

    outs = call(
        functools.partial(state_kernel, n, heads, width),
        [ssm_input, decay_log.T, state_write, skip_scale[None, :]],
        [sds((rows, cols), F32), sds((heads, rows), F32), sds((1, cols), F32)]
        + [sds((size + PAD, piece))] * n,
        [pltpu.VMEM((n, size + PAD, piece), BF)],
    )
    cume, cumt, skip, sends = outs[0], outs[1], outs[2], outs[3:]
    got = exchange(sends, senders=range(n - 1))
    count = min(heads // groups, 8)
    base = []
    for g in range(groups):
        steps = heads // groups // count
        base += call(
            functools.partial(within_kernel, g * steps, steps, count, width),
            [ssm_input, cume, cumt, state_write, state_read, skip],
            [sds((rows, GRP), F32)],
        )
    prior = call(
        functools.partial(prefix_kernel, n),
        got,
        [sds((size, piece))] * n,
        [pltpu.VMEM((n, size + PAD, piece), BF), pltpu.VMEM((n, size, piece), BF)],
    )
    prior = exchange(prior, receivers=range(1, n))
    placed, table = call(
        functools.partial(route_kernel, n, owned),
        [expert_ids.T, combine_fixed.T],
        [sds((slots, rows)), sds((rows, slots))],
    )
    per_group = GRP // piece
    normed = []
    for g in range(groups):
        normed += call(
            functools.partial(gate_kernel, n, g * per_group, per_group),
            [base[g], cume, gate_input, ssm_gain[None, :], state_read, *prior],
            [sds((rows, GRP))],
            [pltpu.VMEM((n, size, piece), BF)],
        )

    kept, given = share_experts(per, jnp.swapaxes(expert_up, 1, 2), expert_down)
    taken = [lax.ppermute(a, "heads", swap) for a in given]

    table_of = tasks(n)
    blocks = {("O", 0): normed}
    feat_block = out_weight.shape[1]
    ratio = n // nh
    got, where_to = [], []

    right = left = normed
    for s in range(1, n - 1):
        for name, line, perm in (
            ("R", right, [(i, i + 1) for i in range(s - 1, n - 1)]),
            ("L", left, [(i, i - 1) for i in range(1, n - s + 1)]),
        ):
            out = []
            for a in line:
                out.append(lax.ppermute(a, "ctx", perm))
            blocks[name, s] = out
        right, left = blocks["R", s], blocks["L", s]

    def options(slot_of_core):
        keys, choice = [], []
        for i in range(2 * n):
            task = table_of[i // 2][slot_of_core(i % 2)]
            if task is None:
                choice.append(0)
                continue
            if task[:2] not in keys:
                keys.append(task[:2])
            choice.append(keys.index(task[:2]))
        return tuple(choice), [blocks[k] for k in keys]

    def rest(held, entries):
        for xi in range(nx):
            for rr in range(ratio):
                perm = [
                    (cc * nh + 2 * xi + core, to * nh + f // ratio)
                    for cc, core, f, to in entries
                    if f % ratio == rr
                ]
                if perm:
                    got.append(lax.ppermute(held, both, perm))
                    where_to.append((0, rr * feat_block))

    def entries_of(slot_of_core, cores):
        return [
            (cc, k, cc, table_of[cc][slot_of_core(k)][2])
            for cc in range(n)
            for k in cores
            if table_of[cc][slot_of_core(k)] is not None
        ]

    for p in range((n - 2) // 2):
        choice, cands = options(lambda k: 2 * p + 1 - k)
        (sent,) = project(choice, cands, out_weight, None, 1)
        recv = lax.ppermute(sent, "heads", swap)
        choice, cands = options(lambda k: 2 * p + k)
        (held,) = project(choice, cands, out_weight, recv, 1)
        rest(held, entries_of(lambda k: 2 * p + k, (0, 1)))
    choice, cands = options(lambda k: n - 2)
    (own,) = project(choice, cands, out_weight, None, 1)
    perm = [(c * nh + i, c * nh + i - 1) for c in range(1, n - 1) for i in range(1, nh, 2)]
    recv = lax.ppermute(own, both, perm)
    (held,) = fold(own, recv, 1)
    rest(held, entries_of(lambda k: n - 2, (0,)))
    choice, cands = options(lambda k: n - 1)
    (sent,) = project_final(choice, cands, out_weight, far, 0, None, 1)
    recv = lax.ppermute(sent, "heads", swap)
    (held,) = project_final(choice, cands, out_weight, far, 1, recv, 1)
    rest(held, entries_of(lambda k: n - 1, (0,)) + [(1, 1, 0, n - 1), (n - 2, 1, n - 1, 0)])

    wide = lat + SQL
    residual, same, apart = call(
        functools.partial(latent_kernel, tuple(where_to)),
        [residual_in, moe_gain[None, :], down_latent, placed, *got],
        [sds((rows, feats), F32), sds((slots // 2, wide)), sds((slots // 2, wide))],
    )
    recv = lax.ppermute(apart, "heads", swap)
    (total,) = call(merge_kernel, [same, recv], [sds((slots // 2, wide))])
    sends = call(
        functools.partial(dispatch_kernel, n, nx),
        across(total),
        [sds((per * CAP, wide))] * n,
        [pltpu.VMEM((slots // 2, wide), BF)],
    )
    sends = call(
        functools.partial(expert_kernel, n, per, float(feats * nh)),
        [*exchange(sends), *kept, *taken],
        [sds((per * CAP, lat))] * n,
    )
    (mine,) = call(functools.partial(returned_kernel, n), exchange(sends), [sds((slots // 2, lat))])
    (mine,) = call(sum_kernel, across(mine), [sds((slots // 2, lat))])
    other = lax.ppermute(mine, "heads", swap)
    (out,) = call(
        combine_kernel,
        [mine, other, table, residual, up_latent],
        [jax.ShapeDtypeStruct((rows, feats), BF)],
    )
    return out


def solution(mesh):
    placed = (
        P(("groups", "ctx"), "heads"),
        P(("groups", "ctx"), "heads"),
        P(("groups", "ctx"), None),
        P(("groups", "ctx"), None),
        P("heads"),
        P(("groups", "ctx"), "heads"),
        P("heads"),
        P("heads", "ctx"),
        P(("groups", "ctx"), "heads"),
        P("heads"),
        P("heads", None),
        P("ctx", None, "heads"),
        P("ctx", "heads", None),
        P(None, "heads"),
        P(("groups", "ctx"), None),
        P(("groups", "ctx"), None),
    )
    return jax.shard_map(
        local, mesh=mesh, in_specs=placed, out_specs=P(("groups", "ctx"), "heads"), check_vma=False
    )
```

```python
import functools

import jax
import jax.numpy as jnp
from jax import lax
from jax.experimental import pallas as pl
from jax.experimental.pallas import tpu as pltpu
from jax.sharding import PartitionSpec as P


GRP = 1024
CAP = 16
EPS = 1e-05
PAD = 16
SQL = 128
LANES = 128
BF = jnp.bfloat16
F32 = jnp.float32

VM = pl.BlockSpec(memory_space=pltpu.VMEM)
LIMIT = 14 * 2**20


def sds(shape, dtype=BF):
    return pltpu.VMEM(shape, dtype)


def call(body, args, outs, scratch=()):
    args = [pltpu.with_memory_space_constraint(a, pltpu.VMEM) for a in args]
    return pl.pallas_call(
        body,
        in_specs=[VM] * len(args),
        out_specs=[VM] * len(outs),
        out_shape=outs,
        scratch_shapes=scratch,
        compiler_params=pltpu.CompilerParams(vmem_limit_bytes=LIMIT),
    )(*args)


def pick(table, index):
    value = jnp.int32(table[0])
    for i, entry in enumerate(table[1:], 1):
        if entry != table[0]:
            value = jnp.where(index == i, jnp.int32(entry), value)
    return value


def dot(a, b):
    return jnp.dot(a, b, preferred_element_type=F32)


def split(v, terms):
    out = []
    for _ in range(terms):
        part = v.astype(BF)
        out.append(part)
        v = v - part.astype(F32)
    return out


def iota(shape, dim):
    return lax.broadcasted_iota(jnp.int32, shape, dim)


def plan_of(rows, shares):
    units = rows // shares // LANES
    sizes = (1, 2, 2, 2, 1)
    if units % sum(sizes) == 0:
        return tuple(size * units // sum(sizes) * LANES for size in sizes)
    return (LANES,) * units


def tasks(n):
    table = []
    for c in range(n):
        row = [("O", 0, c)]
        for s in range(1, n - 1):
            if c - s >= 0:
                row.append(("R", s, c - s))
            if c + s < n:
                row.append(("L", s, c + s))
        if len(row) < n:
            row.insert(n - 2, None)
        table.append(row)
    return table


def state_kernel(n, heads, width, x_ref, decay_ref, write_ref, scale_ref, cume_ref, cumt_ref, skip_ref, *rest):
    outs, pieces = rest[:n], rest[n]
    rows = x_ref.shape[0]
    cols = heads * width
    piece = cols // n
    c = lax.axis_index("ctx")
    upper = (iota((rows, rows), 0) <= iota((rows, rows), 1)).astype(F32).astype(BF)
    cumt = sum(dot(part, upper) for part in split(decay_ref[...], 3))
    cumt_ref[...] = cumt
    cum = cumt.T
    spread = (iota((heads, cols), 1) // width == iota((heads, cols), 0)).astype(F32).astype(BF)
    cume = sum(dot(part, spread) for part in split(cum, 3))
    cume_ref[...] = cume
    skip_ref[...] = sum(dot(part, spread) for part in split(scale_ref[...], 3))
    last = cume[rows - 1 : rows, :]
    weighted = (jnp.exp(cume - last) * x_ref[...].astype(F32)).astype(BF)
    state = lax.dot_general(
        write_ref[...], weighted, (((0,), (0,)), ((), ())), preferred_element_type=F32
    ).astype(BF)
    size = state.shape[0]
    high, low = split(jnp.exp(-last), 2)
    row = iota((PAD, cols), 0)
    tail = jnp.where(row == 0, high.astype(F32), jnp.where(row == 1, low.astype(F32), 0.0)).astype(BF)
    for q in range(n):
        pieces[q, 0:size, :] = state[:, q * piece : (q + 1) * piece]
        pieces[q, size : size + PAD, :] = tail[:, q * piece : (q + 1) * piece]
    for k in range(n):
        outs[k][...] = pieces[c ^ k]


def prefix_kernel(n, *refs):
    ins, outs, got, made = refs[:n], refs[n : 2 * n], refs[2 * n], refs[2 * n + 1]
    c = lax.axis_index("ctx")
    size = outs[0].shape[0]
    for k in range(n):
        got[c ^ k] = ins[k][...]
    total = jnp.zeros(outs[0].shape, F32)
    for j in range(n):
        made[j] = total.astype(BF)
        if j < n - 1:
            keep = got[j, size : size + PAD, :].astype(F32)
            keep = keep[0:1, :] + keep[1:2, :]
            total = total * keep + got[j, 0:size, :].astype(F32)
    for k in range(n):
        outs[k][...] = made[c ^ k]


def within_kernel(first, steps, count, width, x_ref, cume_ref, cumt_ref, write_ref, read_ref, skip_ref, out_ref):
    rows = x_ref.shape[0]
    half = rows // 2
    inter = lax.dot_general(
        read_ref[...], write_ref[...], (((1,), (1,)), ((), ())), preferred_element_type=F32
    )
    causal = iota((half, half), 0) >= iota((half, half), 1)
    block = count * width

    def step(i, carry):
        start = pl.multiple_of((first + i) * block, block)
        x_all = x_ref[:, pl.ds(start, block)]
        cume = cume_ref[:, pl.ds(start, block)]
        skip_all = skip_ref[:, pl.ds(start, block)]
        results = []
        for j in range(count):
            lanes = slice(j * width, (j + 1) * width)
            x = x_all[:, lanes]
            col = cume[:, j * width : j * width + 1]
            line = cumt_ref[pl.ds((first + i) * count + j, 1), :]
            top, bottom = col[0:half], col[half:rows]
            left, right = line[:, 0:half], line[:, half:rows]
            m00 = jnp.exp(jnp.where(causal, left - top, 0.0))
            m00 = jnp.where(causal, m00 * inter[0:half, 0:half], 0.0).astype(BF)
            m10 = (jnp.exp(left - bottom) * inter[half:rows, 0:half]).astype(BF)
            m11 = jnp.exp(jnp.where(causal, right - bottom, 0.0))
            m11 = jnp.where(causal, m11 * inter[half:rows, half:rows], 0.0).astype(BF)
            upper = dot(m00, x[0:half])
            lower = dot(m10, x[0:half]) + dot(m11, x[half:rows])
            results.append(jnp.concatenate([upper, lower], axis=0))
        result = results[0] if count == 1 else jnp.concatenate(results, axis=1)
        at = pl.ds(pl.multiple_of(i * block, block), block)
        out_ref[:, at] = result + skip_all * x_all.astype(F32)
        return carry

    lax.fori_loop(0, steps, step, 0)


def gate_kernel(n, base, per, base_ref, cume_ref, gate_ref, gain_ref, read_ref, *refs):
    ins, out_ref, prior = refs[:n], refs[n], refs[n + 1]
    c = lax.axis_index("ctx")
    at = slice(base * (GRP // per), (base + per) * (GRP // per))
    for k in range(n):
        prior[c ^ k] = ins[k][...]
    reads = read_ref[...]
    carried = [dot(reads, prior[base + q]) for q in range(per)]
    carried = carried[0] if per == 1 else jnp.concatenate(carried, axis=1)
    mixed = base_ref[...] + carried * jnp.exp(-cume_ref[:, at])
    gate = gate_ref[:, at].astype(F32)
    gated = mixed * (gate / (1.0 + jnp.exp(-gate)))
    mean = jnp.mean(gated * gated, axis=1, keepdims=True)
    out_ref[...] = (gated * lax.rsqrt(mean + EPS) * gain_ref[:, at]).astype(BF)


def load_rows(choice, index, options, groups, cands, a):
    grp = a.shape[1] // groups
    sel = pick(choice, index)
    for o in range(options):

        def copy(o=o):
            for g in range(groups):
                a[:, g * grp : (g + 1) * grp] = cands[o * groups + g][...]

        if len(set(choice)) == 1:
            if o == choice[0]:
                copy()
        else:
            pl.when(sel == o)(copy)


def store_parts(total, outs):
    total = total.astype(BF)
    if len(outs) == 2:
        half = total.shape[0] // 2
        first = lax.rem(lax.axis_index("heads") // 2, 2) == 0
        outs[0][...] = jnp.where(first, total[:half], total[half:])
        outs[1][...] = jnp.where(first, total[half:], total[:half])
    else:
        outs[0][...] = total


def project_kernel(choice, options, groups, fold, parts, *refs):
    cands, refs = refs[: options * groups], refs[options * groups :]
    w_ref, refs = refs[0], refs[1:]
    if fold:
        add_ref, refs = refs[0], refs[1:]
    outs, a = refs[:parts], refs[parts]
    place = lax.axis_index("ctx") * 2 + lax.rem(lax.axis_index("heads"), 2)
    load_rows(choice, place, options, groups, cands, a)
    total = dot(a[...], w_ref[...])
    if fold:
        total = total + add_ref[...].astype(F32)
    store_parts(total, outs)


def far_kernel(choice, options, groups, shares, chunks, *refs):
    cands, refs = refs[: options * groups], refs[options * groups :]
    *far, out_ref, a = refs
    place = lax.axis_index("ctx") * 2 + lax.rem(lax.axis_index("heads"), 2)
    load_rows(choice, place, options, groups, cands, a)
    plan = [ref.shape[0] for ref in far[: chunks - 1]]
    plan.append(far[chunks - 1].shape[0] // shares)
    total = None
    for k in range(shares):
        share = lax.axis_index("groups") ^ k
        for j in range(chunks):
            start = pl.multiple_of(share * sum(plan) + sum(plan[:j]), LANES)
            if j == chunks - 1:
                weight = far[j][k * plan[j] : (k + 1) * plan[j], :]
            elif k == 0:
                weight = far[j][...]
            else:
                weight = far[chunks + (k - 1) * (chunks - 1) + j][...]
            part = dot(a[:, pl.ds(start, plan[j])], weight)
            total = part if total is None else total + part
    out_ref[...] = total.astype(BF)


def project(choice, cands, weight, add, parts):
    options, groups = len(cands), len(cands[0])
    rows, grp = cands[0][0].shape
    args = [a for cand in cands for a in cand] + [weight]
    if add is not None:
        args.append(add)
    return call(
        functools.partial(project_kernel, choice, options, groups, add is not None, parts),
        args,
        [sds((rows // parts, weight.shape[1]))] * parts,
        [pltpu.VMEM((rows, groups * grp), BF)],
    )


def project_far(choice, cands, far):
    options, groups = len(cands), len(cands[0])
    rows, grp = cands[0][0].shape
    return call(
        functools.partial(far_kernel, choice, options, groups, len(far), len(far[0])),
        [a for cand in cands for a in cand] + [a for share in far for a in share],
        [sds((rows, far[0][0].shape[1]))],
        [pltpu.VMEM((rows, groups * grp), BF)],
    )


def fold_kernel(own_ref, add_ref, *outs):
    store_parts(own_ref[...].astype(F32) + add_ref[...].astype(F32), outs)


def fold(own, add, parts):
    shape = (own.shape[0] // parts, own.shape[1])
    return call(fold_kernel, [own, add], [sds(shape)] * parts)


def cut_kernel(plan, picks, w_ref, *refs):
    outs, sem = refs[:-1], refs[-1]
    copies = []
    for j, out in zip(picks, outs):
        for k in range(out.shape[0] // plan[j]):
            share = (lax.axis_index("groups") ^ k) * sum(plan)
            start = pl.multiple_of(share + sum(plan[:j]), LANES)
            source = w_ref.at[pl.ds(start, plan[j]), :]
            target = out.at[pl.ds(k * plan[j], plan[j]), :]
            copies.append(pltpu.make_async_copy(source, target, sem.at[len(copies)]))
    for copy in copies:
        copy.start()
    for copy in copies:
        copy.wait()


def cut(weight, space, plan, picks):
    shares = weight.shape[0] // sum(plan)
    sizes = [plan[j] * (shares if j == len(plan) - 1 else 1) for j in picks]
    return pl.pallas_call(
        functools.partial(cut_kernel, plan, picks),
        in_specs=[pl.BlockSpec(memory_space=space)],
        out_specs=[VM] * len(picks),
        out_shape=[sds((size, weight.shape[1])) for size in sizes],
        scratch_shapes=[pltpu.SemaphoreType.DMA((shares * len(picks),))],
        compiler_params=pltpu.CompilerParams(vmem_limit_bytes=LIMIT),
        name="cut",
    )(pltpu.with_memory_space_constraint(weight, space))


def route_kernel(owners, owned, ids_ref, fixed_ref, placed_ref, table_ref):
    named, rows = ids_ref.shape
    wave = owners * owned
    ids, fixed = ids_ref[...], fixed_ref[...]
    line = iota((wave, rows), 0)
    chosen = jnp.zeros((wave, rows), jnp.int32)
    weight = jnp.zeros((wave, rows), jnp.int32)
    for k in range(named):
        match = ids[k : k + 1, :] == line
        chosen = jnp.where(match, 1, chosen)
        weight = weight + jnp.where(match, fixed[k : k + 1, :], 0)
    chosen = chosen.astype(F32)
    upper = (iota((rows, rows), 0) <= iota((rows, rows), 1)).astype(F32).astype(BF)
    slot = dot(chosen.astype(BF), upper) - 1.0
    slot = jnp.where(chosen > 0.5, slot, -1.0).astype(BF)
    route = (weight.astype(F32) / 65536.0).astype(BF)
    slots = wave * CAP
    per = owned // 2
    s = iota((slots, wave), 0) // CAP
    expert = (s // per % owners) * owned + s // (per * owners) * per + s % per
    spread = (expert == iota((slots, wave), 1)).astype(F32).astype(BF)
    placed = dot(spread, slot) == (iota((slots, rows), 0) % CAP).astype(F32)
    table_ref[...] = jnp.where(placed, dot(spread, route), 0.0).T.astype(BF)
    placed_ref[...] = jnp.where(placed, 1.0, 0.0).astype(BF)


def by_core(value):
    half = value.shape[0] // 2
    first = lax.rem(lax.axis_index("heads"), 2) == 0
    mine = jnp.where(first, value[:half], value[half:])
    other = jnp.where(first, value[half:], value[:half])
    return mine, other


def squares_block(value):
    high, low = split(value, 2)
    lane = iota((value.shape[0], SQL), 1)
    high, low = high.astype(F32), low.astype(F32)
    return jnp.where(lane == 0, high, jnp.where(lane == 1, low, 0.0)).astype(BF)


def latent_kernel(where_to, resin_ref, gain_ref, down_ref, placed_ref, *refs):
    count = len(where_to)
    ins = refs[:count]
    res_ref, same_ref, other_ref = refs[count:]
    done = set()
    for (r0, c0), ref in zip(where_to, ins):
        at = (slice(r0, r0 + ref.shape[0]), slice(c0, c0 + ref.shape[1]))
        value = ref[...].astype(F32)
        if (r0, c0) in done:
            res_ref[at] += value
        else:
            res_ref[at] = value + resin_ref[at].astype(F32)
            done.add((r0, c0))
    residual = res_ref[...]
    placed = placed_ref[...]
    scaled = dot(placed, (residual * gain_ref[...]).astype(BF)).astype(BF)
    squares = jnp.sum(residual * residual, axis=1, keepdims=True)
    squares = dot(placed, squares_block(squares)).astype(BF)
    lat = down_ref.shape[1]
    mine, other = by_core(dot(scaled, down_ref[...]))
    same_ref[:, :lat] = mine.astype(BF)
    other_ref[:, :lat] = other.astype(BF)
    mine, other = by_core(squares)
    same_ref[:, lat:] = mine
    other_ref[:, lat:] = other


def add_up(ins, total):
    lat = total.shape[1] - SQL
    total[:, :lat] = sum(ref[:, :lat].astype(F32) for ref in ins).astype(BF)
    squares = sum(ref[:, lat:].astype(F32) for ref in ins)
    total[:, lat:] = squares_block(squares[:, 0:1] + squares[:, 1:2])


def merge_kernel(own_ref, recv_ref, out_ref):
    add_up((own_ref, recv_ref), out_ref)


def dispatch_kernel(n, count, *refs):
    ins, outs, total = refs[:count], refs[count : count + n], refs[count + n]
    c = lax.axis_index("ctx")
    rows = outs[0].shape[0]
    add_up(ins, total)
    for k in range(n):
        start = pl.multiple_of((c ^ k) * rows, rows)
        outs[k][...] = total[pl.ds(start, rows), :]


def expert_kernel(n, per, features, *refs):
    ins = refs[:n]
    kept_ref, taken_ref = refs[n : n + 2]
    outs = refs[n + 2 :]
    lat = outs[0].shape[1]
    contract = (((1,), (1,)), ((), ()))
    for j in range(per):
        rows = jnp.concatenate([ref[j * CAP : (j + 1) * CAP, :] for ref in ins], axis=0)
        square = rows[:, lat : lat + 1].astype(F32) + rows[:, lat + 1 : lat + 2].astype(F32)
        rows = (rows[:, :lat].astype(F32) * lax.rsqrt(square / features + EPS)).astype(BF)
        result = None
        for ref in (kept_ref, taken_ref):
            up, down = ref[j], ref[per + j]
            hidden = lax.dot_general(rows, up, contract, preferred_element_type=F32)
            hidden = jnp.maximum(hidden, 0.0)
            part = dot((hidden * hidden).astype(BF), down)
            result = part if result is None else result + part
        result = result.astype(BF)
        for k in range(n):
            outs[k][j * CAP : (j + 1) * CAP, :] = result[k * CAP : (k + 1) * CAP, :]


def share_kernel(per, up_ref, down_ref, kept_ref, given_ref, sem):
    core = lax.rem(lax.axis_index("heads"), 2)
    copies = []
    for i, ref in enumerate((up_ref, down_ref)):
        for k, (start, out) in enumerate(((core * per, kept_ref), ((1 - core) * per, given_ref))):
            copies.append(
                pltpu.make_async_copy(
                    ref.at[pl.ds(start, per)], out.at[pl.ds(i * per, per)], sem.at[2 * i + k]
                )
            )
    for copy in copies:
        copy.start()
    for copy in copies:
        copy.wait()


def share_experts(per, up, down):
    return pl.pallas_call(
        functools.partial(share_kernel, per),
        in_specs=[pl.BlockSpec(memory_space=pl.ANY)] * 2,
        out_specs=[VM] * 2,
        out_shape=[sds((2 * per, *up.shape[1:]))] * 2,
        scratch_shapes=[pltpu.SemaphoreType.DMA((4,))],
        compiler_params=pltpu.CompilerParams(vmem_limit_bytes=LIMIT),
        name="share",
    )(up, down)


def returned_kernel(n, *refs):
    ins, out_ref = refs[:n], refs[n]
    c = lax.axis_index("ctx")
    rows = ins[0].shape[0]
    for k in range(n):
        out_ref[pl.ds(pl.multiple_of((c ^ k) * rows, rows), rows), :] = ins[k][...]


def sum_kernel(*refs):
    refs[-1][...] = sum(ref[...].astype(F32) for ref in refs[:-1]).astype(BF)


def combine_kernel(mine_ref, other_ref, table_ref, res_ref, up_ref, out_ref):
    mine, other = mine_ref[...], other_ref[...]
    first = lax.rem(lax.axis_index("heads"), 2) == 0
    table = table_ref[...]
    half = table.shape[1] // 2
    combined = dot(table[:, :half], jnp.where(first, mine, other))
    combined = combined + dot(table[:, half:], jnp.where(first, other, mine))
    out_ref[...] = (res_ref[...] + dot(combined.astype(BF), up_ref[...])).astype(BF)


def local(
    ssm_input,
    decay_log,
    state_write,
    state_read,
    skip_scale,
    gate_input,
    ssm_gain,
    out_weight,
    residual_in,
    moe_gain,
    down_latent,
    expert_up,
    expert_down,
    up_latent,
    expert_ids,
    combine_fixed,
):
    n, nh = lax.axis_size("ctx"), lax.axis_size("heads")
    nx, ny = nh // 2, lax.axis_size("groups")
    both = ("ctx", "heads")
    rows, cols = ssm_input.shape
    heads = decay_log.shape[1]
    width = cols // heads
    size = state_write.shape[1]
    groups = cols // GRP
    piece = cols // n
    feats = residual_in.shape[1]
    owned = expert_up.shape[0]
    per = owned // 2
    slots = owned * n * CAP
    lat = down_latent.shape[1]
    swap = [(i, i ^ 1) for i in range(nh)]

    def exchange(arrays, senders=range(n), receivers=range(n)):
        out = [arrays[0]]
        for k in range(1, n):
            perm = [(i, i ^ k) for i in senders if i ^ k in receivers]
            out.append(lax.ppermute(arrays[k], "ctx", perm))
        return out

    def across(a):
        out = [a]
        for k in range(1, nx):
            out.append(lax.ppermute(a, "heads", [(i, i ^ (2 * k)) for i in range(nh)]))
        return out

    plan = plan_of(out_weight.shape[0], ny)
    chunks = cut(out_weight, pltpu.HBM, plan, range(1))
    chunks = chunks + cut(out_weight, pl.ANY, plan, range(1, len(plan)))
    far = [[] for _ in range(ny)]
    for j, chunk in enumerate(chunks):
        far[0].append(lax.ppermute(chunk, "ctx", [(0, 1), (n - 1, n - 2)]))
        for k in range(1, ny if j < len(plan) - 1 else 1):
            perm = []
            for y in range(ny):
                perm += [(y * n + c, (y ^ k) * n + c) for c in (1, n - 2)]
            far[k].append(lax.ppermute(far[0][j], ("groups", "ctx"), perm))

    outs = call(
        functools.partial(state_kernel, n, heads, width),
        [ssm_input, decay_log.T, state_write, skip_scale[None, :]],
        [sds((rows, cols), F32), sds((heads, rows), F32), sds((1, cols), F32)]
        + [sds((size + PAD, piece))] * n,
        [pltpu.VMEM((n, size + PAD, piece), BF)],
    )
    cume, cumt, skip, sends = outs[0], outs[1], outs[2], outs[3:]
    got = exchange(sends, senders=range(n - 1))
    count = min(heads // groups, 8)
    base = []
    for g in range(groups):
        steps = heads // groups // count
        base += call(
            functools.partial(within_kernel, g * steps, steps, count, width),
            [ssm_input, cume, cumt, state_write, state_read, skip],
            [sds((rows, GRP), F32)],
        )
    prior = call(
        functools.partial(prefix_kernel, n),
        got,
        [sds((size, piece))] * n,
        [pltpu.VMEM((n, size + PAD, piece), BF), pltpu.VMEM((n, size, piece), BF)],
    )
    prior = exchange(prior, receivers=range(1, n))
    placed, table = call(
        functools.partial(route_kernel, n, owned),
        [expert_ids.T, combine_fixed.T],
        [sds((slots, rows)), sds((rows, slots))],
    )
    per_group = GRP // piece
    normed = []
    for g in range(groups):
        normed += call(
            functools.partial(gate_kernel, n, g * per_group, per_group),
            [base[g], cume, gate_input, ssm_gain[None, :], state_read, *prior],
            [sds((rows, GRP))],
            [pltpu.VMEM((n, size, piece), BF)],
        )

    kept, given = share_experts(per, jnp.swapaxes(expert_up, 1, 2), expert_down)
    taken = lax.ppermute(given, "heads", swap)

    table_of = tasks(n)
    blocks = {("O", 0): normed}
    feat_block = out_weight.shape[1]
    ratio = n // nh
    got, where_to = [], []

    right = left = normed
    for s in range(1, n - 1):
        for name, line, perm in (
            ("R", right, [(i, i + 1) for i in range(s - 1, n - 1)]),
            ("L", left, [(i, i - 1) for i in range(1, n - s + 1)]),
        ):
            out = []
            for a in line:
                out.append(lax.ppermute(a, "ctx", perm))
            blocks[name, s] = out
        right, left = blocks["R", s], blocks["L", s]

    def options(slot_of_core):
        keys, choice = [], []
        for i in range(2 * n):
            task = table_of[i // 2][slot_of_core(i % 2)]
            if task is None:
                choice.append(0)
                continue
            if task[:2] not in keys:
                keys.append(task[:2])
            choice.append(keys.index(task[:2]))
        return tuple(choice), [blocks[k] for k in keys]

    def rest(held, entries):
        for xi in range(nx):
            for rr in range(ratio):
                perm = [
                    (cc * nh + 2 * xi + core, to * nh + f // ratio)
                    for cc, core, f, to in entries
                    if f % ratio == rr
                ]
                if perm:
                    got.append(lax.ppermute(held, both, perm))
                    where_to.append((0, rr * feat_block))

    def entries_of(slot_of_core, cores):
        return [
            (cc, k, cc, table_of[cc][slot_of_core(k)][2])
            for cc in range(n)
            for k in cores
            if table_of[cc][slot_of_core(k)] is not None
        ]

    for p in range((n - 2) // 2):
        choice, cands = options(lambda k: 2 * p + 1 - k)
        (sent,) = project(choice, cands, out_weight, None, 1)
        recv = lax.ppermute(sent, "heads", swap)
        choice, cands = options(lambda k: 2 * p + k)
        (held,) = project(choice, cands, out_weight, recv, 1)
        rest(held, entries_of(lambda k: 2 * p + k, (0, 1)))
    for i, keeper in ((n - 2, 0), (n - 1, 1)):
        choice, cands = options(lambda k: i)
        (own,) = project(choice, cands, out_weight, None, 1)
        recv = lax.ppermute(own, "heads", swap)
        (held,) = fold(own, recv, 1)
        rest(held, entries_of(lambda k: i, (keeper,)))
    choice, cands = options(lambda k: n - 1)
    (own,) = project_far(choice, cands, far)
    recv = lax.ppermute(own, "heads", swap)
    (held,) = fold(own, recv, 1)
    rest(held, [(1, 0, 0, n - 1), (n - 2, 0, n - 1, 0)])

    wide = lat + SQL
    residual, same, apart = call(
        functools.partial(latent_kernel, tuple(where_to)),
        [residual_in, moe_gain[None, :], down_latent, placed, *got],
        [sds((rows, feats), F32), sds((slots // 2, wide)), sds((slots // 2, wide))],
    )
    recv = lax.ppermute(apart, "heads", swap)
    (total,) = call(merge_kernel, [same, recv], [sds((slots // 2, wide))])
    sends = call(
        functools.partial(dispatch_kernel, n, nx),
        across(total),
        [sds((per * CAP, wide))] * n,
        [pltpu.VMEM((slots // 2, wide), BF)],
    )
    sends = call(
        functools.partial(expert_kernel, n, per, float(feats * nh)),
        [*exchange(sends), kept, taken],
        [sds((per * CAP, lat))] * n,
    )
    (mine,) = call(functools.partial(returned_kernel, n), exchange(sends), [sds((slots // 2, lat))])
    (mine,) = call(sum_kernel, across(mine), [sds((slots // 2, lat))])
    other = lax.ppermute(mine, "heads", swap)
    (out,) = call(
        combine_kernel,
        [mine, other, table, residual, up_latent],
        [jax.ShapeDtypeStruct((rows, feats), BF)],
    )
    return out


def solution(mesh):
    placed = (
        P(("groups", "ctx"), "heads"),
        P(("groups", "ctx"), "heads"),
        P(("groups", "ctx"), None),
        P(("groups", "ctx"), None),
        P("heads"),
        P(("groups", "ctx"), "heads"),
        P("heads"),
        P("heads", "ctx"),
        P(("groups", "ctx"), "heads"),
        P("heads"),
        P("heads", None),
        P("ctx", None, "heads"),
        P("ctx", "heads", None),
        P(None, "heads"),
        P(("groups", "ctx"), None),
        P(("groups", "ctx"), None),
    )
    return jax.shard_map(
        local, mesh=mesh, in_specs=placed, out_specs=P(("groups", "ctx"), "heads"), check_vma=False
    )
```

```python
import functools

import jax
import jax.numpy as jnp
from jax import lax
from jax.experimental import pallas as pl
from jax.experimental.pallas import tpu as pltpu
from jax.sharding import PartitionSpec as P


GRP = 1024
CAP = 16
EPS = 1e-05
PAD = 16
SQL = 128
LANES = 128
BF = jnp.bfloat16
F32 = jnp.float32

VM = pl.BlockSpec(memory_space=pltpu.VMEM)
LIMIT = 14 * 2**20


def sds(shape, dtype=BF):
    return pltpu.VMEM(shape, dtype)


def call(body, args, outs, scratch=()):
    args = [pltpu.with_memory_space_constraint(a, pltpu.VMEM) for a in args]
    return pl.pallas_call(
        body,
        in_specs=[VM] * len(args),
        out_specs=[VM] * len(outs),
        out_shape=outs,
        scratch_shapes=scratch,
        compiler_params=pltpu.CompilerParams(vmem_limit_bytes=LIMIT),
    )(*args)


def pick(table, index):
    value = jnp.int32(table[0])
    for i, entry in enumerate(table[1:], 1):
        if entry != table[0]:
            value = jnp.where(index == i, jnp.int32(entry), value)
    return value


def dot(a, b):
    return jnp.dot(a, b, preferred_element_type=F32)


def split(v, terms):
    out = []
    for _ in range(terms):
        part = v.astype(BF)
        out.append(part)
        v = v - part.astype(F32)
    return out


def iota(shape, dim):
    return lax.broadcasted_iota(jnp.int32, shape, dim)


def plan_of(rows, shares):
    units = rows // shares // LANES
    sizes = (1, 2, 2, 2, 1)
    if units % sum(sizes) == 0:
        return tuple(size * units // sum(sizes) * LANES for size in sizes)
    return (LANES,) * units


def tasks(n):
    table = []
    for c in range(n):
        row = [("O", 0, c)]
        for s in range(1, n - 1):
            if c - s >= 0:
                row.append(("R", s, c - s))
            if c + s < n:
                row.append(("L", s, c + s))
        if len(row) < n:
            row.insert(n - 2, None)
        table.append(row)
    return table


def state_kernel(n, heads, width, x_ref, decay_ref, write_ref, scale_ref, cume_ref, cumt_ref, skip_ref, *rest):
    outs, pieces = rest[:n], rest[n]
    rows = x_ref.shape[0]
    cols = heads * width
    piece = cols // n
    c = lax.axis_index("ctx")
    upper = (iota((rows, rows), 0) <= iota((rows, rows), 1)).astype(F32).astype(BF)
    cumt = sum(dot(part, upper) for part in split(decay_ref[...], 3))
    cumt_ref[...] = cumt
    cum = cumt.T
    spread = (iota((heads, cols), 1) // width == iota((heads, cols), 0)).astype(F32).astype(BF)
    cume = sum(dot(part, spread) for part in split(cum, 3))
    cume_ref[...] = cume
    skip_ref[...] = sum(dot(part, spread) for part in split(scale_ref[...], 3))
    last = cume[rows - 1 : rows, :]
    weighted = (jnp.exp(cume - last) * x_ref[...].astype(F32)).astype(BF)
    state = lax.dot_general(
        write_ref[...], weighted, (((0,), (0,)), ((), ())), preferred_element_type=F32
    ).astype(BF)
    size = state.shape[0]
    high, low = split(jnp.exp(-last), 2)
    row = iota((PAD, cols), 0)
    tail = jnp.where(row == 0, high.astype(F32), jnp.where(row == 1, low.astype(F32), 0.0)).astype(BF)
    for q in range(n):
        pieces[q, 0:size, :] = state[:, q * piece : (q + 1) * piece]
        pieces[q, size : size + PAD, :] = tail[:, q * piece : (q + 1) * piece]
    for k in range(n):
        outs[k][...] = pieces[c ^ k]


def prefix_kernel(n, *refs):
    ins, outs, got, made = refs[:n], refs[n : 2 * n], refs[2 * n], refs[2 * n + 1]
    c = lax.axis_index("ctx")
    size = outs[0].shape[0]
    for k in range(n):
        got[c ^ k] = ins[k][...]
    total = jnp.zeros(outs[0].shape, F32)
    for j in range(n):
        made[j] = total.astype(BF)
        if j < n - 1:
            keep = got[j, size : size + PAD, :].astype(F32)
            keep = keep[0:1, :] + keep[1:2, :]
            total = total * keep + got[j, 0:size, :].astype(F32)
    for k in range(n):
        outs[k][...] = made[c ^ k]


def within_kernel(first, steps, count, width, x_ref, cume_ref, cumt_ref, write_ref, read_ref, skip_ref, out_ref):
    rows = x_ref.shape[0]
    half = rows // 2
    inter = lax.dot_general(
        read_ref[...], write_ref[...], (((1,), (1,)), ((), ())), preferred_element_type=F32
    )
    causal = iota((half, half), 0) >= iota((half, half), 1)
    block = count * width

    def step(i, carry):
        start = pl.multiple_of((first + i) * block, block)
        x_all = x_ref[:, pl.ds(start, block)]
        cume = cume_ref[:, pl.ds(start, block)]
        skip_all = skip_ref[:, pl.ds(start, block)]
        results = []
        for j in range(count):
            lanes = slice(j * width, (j + 1) * width)
            x = x_all[:, lanes]
            col = cume[:, j * width : j * width + 1]
            line = cumt_ref[pl.ds((first + i) * count + j, 1), :]
            top, bottom = col[0:half], col[half:rows]
            left, right = line[:, 0:half], line[:, half:rows]
            m00 = jnp.exp(jnp.where(causal, left - top, 0.0))
            m00 = jnp.where(causal, m00 * inter[0:half, 0:half], 0.0).astype(BF)
            m10 = (jnp.exp(left - bottom) * inter[half:rows, 0:half]).astype(BF)
            m11 = jnp.exp(jnp.where(causal, right - bottom, 0.0))
            m11 = jnp.where(causal, m11 * inter[half:rows, half:rows], 0.0).astype(BF)
            upper = dot(m00, x[0:half])
            lower = dot(m10, x[0:half]) + dot(m11, x[half:rows])
            results.append(jnp.concatenate([upper, lower], axis=0))
        result = results[0] if count == 1 else jnp.concatenate(results, axis=1)
        at = pl.ds(pl.multiple_of(i * block, block), block)
        out_ref[:, at] = result + skip_all * x_all.astype(F32)
        return carry

    lax.fori_loop(0, steps, step, 0)


def gate_kernel(n, base, per, base_ref, cume_ref, gate_ref, gain_ref, read_ref, *refs):
    ins, out_ref, prior = refs[:n], refs[n], refs[n + 1]
    c = lax.axis_index("ctx")
    at = slice(base * (GRP // per), (base + per) * (GRP // per))
    for k in range(n):
        prior[c ^ k] = ins[k][...]
    reads = read_ref[...]
    carried = [dot(reads, prior[base + q]) for q in range(per)]
    carried = carried[0] if per == 1 else jnp.concatenate(carried, axis=1)
    mixed = base_ref[...] + carried * jnp.exp(-cume_ref[:, at])
    gate = gate_ref[:, at].astype(F32)
    gated = mixed * (gate / (1.0 + jnp.exp(-gate)))
    mean = jnp.mean(gated * gated, axis=1, keepdims=True)
    out_ref[...] = (gated * lax.rsqrt(mean + EPS) * gain_ref[:, at]).astype(BF)


def load_rows(choice, index, options, groups, cands, a):
    grp = a.shape[1] // groups
    sel = pick(choice, index)
    for o in range(options):

        def copy(o=o):
            for g in range(groups):
                a[:, g * grp : (g + 1) * grp] = cands[o * groups + g][...]

        if len(set(choice)) == 1:
            if o == choice[0]:
                copy()
        else:
            pl.when(sel == o)(copy)


def store_parts(total, outs):
    total = total.astype(BF)
    if len(outs) == 2:
        half = total.shape[0] // 2
        first = lax.rem(lax.axis_index("heads") // 2, 2) == 0
        outs[0][...] = jnp.where(first, total[:half], total[half:])
        outs[1][...] = jnp.where(first, total[half:], total[:half])
    else:
        outs[0][...] = total


def project_kernel(choice, options, groups, fold, parts, *refs):
    cands, refs = refs[: options * groups], refs[options * groups :]
    w_ref, refs = refs[0], refs[1:]
    if fold:
        add_ref, refs = refs[0], refs[1:]
    outs, a = refs[:parts], refs[parts]
    place = lax.axis_index("ctx") * 2 + lax.rem(lax.axis_index("heads"), 2)
    load_rows(choice, place, options, groups, cands, a)
    total = dot(a[...], w_ref[...])
    if fold:
        total = total + add_ref[...].astype(F32)
    store_parts(total, outs)


def far_kernel(choice, options, groups, shares, chunks, *refs):
    cands, refs = refs[: options * groups], refs[options * groups :]
    *far, out_ref, a = refs
    place = lax.axis_index("ctx") * 2 + lax.rem(lax.axis_index("heads"), 2)
    load_rows(choice, place, options, groups, cands, a)
    plan = [ref.shape[0] for ref in far[: chunks - 1]]
    plan.append(far[chunks - 1].shape[0] // shares)
    total = None
    for k in range(shares):
        share = lax.axis_index("groups") ^ k
        for j in range(chunks):
            start = pl.multiple_of(share * sum(plan) + sum(plan[:j]), LANES)
            if j == chunks - 1:
                weight = far[j][k * plan[j] : (k + 1) * plan[j], :]
            elif k == 0:
                weight = far[j][...]
            else:
                weight = far[chunks + (k - 1) * (chunks - 1) + j][...]
            part = dot(a[:, pl.ds(start, plan[j])], weight)
            total = part if total is None else total + part
    out_ref[...] = total.astype(BF)


def project(choice, cands, weight, add, parts):
    options, groups = len(cands), len(cands[0])
    rows, grp = cands[0][0].shape
    args = [a for cand in cands for a in cand] + [weight]
    if add is not None:
        args.append(add)
    return call(
        functools.partial(project_kernel, choice, options, groups, add is not None, parts),
        args,
        [sds((rows // parts, weight.shape[1]))] * parts,
        [pltpu.VMEM((rows, groups * grp), BF)],
    )


def project_far(choice, cands, far):
    options, groups = len(cands), len(cands[0])
    rows, grp = cands[0][0].shape
    return call(
        functools.partial(far_kernel, choice, options, groups, len(far), len(far[0])),
        [a for cand in cands for a in cand] + [a for share in far for a in share],
        [sds((rows, far[0][0].shape[1]))],
        [pltpu.VMEM((rows, groups * grp), BF)],
    )


def fold_kernel(own_ref, add_ref, *outs):
    store_parts(own_ref[...].astype(F32) + add_ref[...].astype(F32), outs)


def fold(own, add, parts):
    shape = (own.shape[0] // parts, own.shape[1])
    return call(fold_kernel, [own, add], [sds(shape)] * parts)


def cut_kernel(plan, picks, w_ref, *refs):
    outs, sem = refs[:-1], refs[-1]
    copies = []
    for j, out in zip(picks, outs):
        for k in range(out.shape[0] // plan[j]):
            share = (lax.axis_index("groups") ^ k) * sum(plan)
            start = pl.multiple_of(share + sum(plan[:j]), LANES)
            source = w_ref.at[pl.ds(start, plan[j]), :]
            target = out.at[pl.ds(k * plan[j], plan[j]), :]
            copies.append(pltpu.make_async_copy(source, target, sem.at[len(copies)]))
    for copy in copies:
        copy.start()
    for copy in copies:
        copy.wait()


def cut(weight, space, plan, picks):
    shares = weight.shape[0] // sum(plan)
    sizes = [plan[j] * (shares if j == len(plan) - 1 else 1) for j in picks]
    return pl.pallas_call(
        functools.partial(cut_kernel, plan, picks),
        in_specs=[pl.BlockSpec(memory_space=space)],
        out_specs=[VM] * len(picks),
        out_shape=[sds((size, weight.shape[1])) for size in sizes],
        scratch_shapes=[pltpu.SemaphoreType.DMA((shares * len(picks),))],
        compiler_params=pltpu.CompilerParams(vmem_limit_bytes=LIMIT),
        name="cut",
    )(pltpu.with_memory_space_constraint(weight, space))


def route_kernel(owners, owned, ids_ref, fixed_ref, placed_ref, table_ref):
    named, rows = ids_ref.shape
    wave = owners * owned
    ids, fixed = ids_ref[...], fixed_ref[...]
    line = iota((wave, rows), 0)
    chosen = jnp.zeros((wave, rows), jnp.int32)
    weight = jnp.zeros((wave, rows), jnp.int32)
    for k in range(named):
        match = ids[k : k + 1, :] == line
        chosen = jnp.where(match, 1, chosen)
        weight = weight + jnp.where(match, fixed[k : k + 1, :], 0)
    chosen = chosen.astype(F32)
    upper = (iota((rows, rows), 0) <= iota((rows, rows), 1)).astype(F32).astype(BF)
    slot = dot(chosen.astype(BF), upper) - 1.0
    slot = jnp.where(chosen > 0.5, slot, -1.0).astype(BF)
    route = (weight.astype(F32) / 65536.0).astype(BF)
    slots = wave * CAP
    per = owned // 2
    s = iota((slots, wave), 0) // CAP
    expert = (s // per % owners) * owned + s // (per * owners) * per + s % per
    spread = (expert == iota((slots, wave), 1)).astype(F32).astype(BF)
    placed = dot(spread, slot) == (iota((slots, rows), 0) % CAP).astype(F32)
    table_ref[...] = jnp.where(placed, dot(spread, route), 0.0).T.astype(BF)
    placed_ref[...] = jnp.where(placed, 1.0, 0.0).astype(BF)


def by_core(value):
    half = value.shape[0] // 2
    first = lax.rem(lax.axis_index("heads"), 2) == 0
    mine = jnp.where(first, value[:half], value[half:])
    other = jnp.where(first, value[half:], value[:half])
    return mine, other


def squares_block(value):
    high, low = split(value, 2)
    lane = iota((value.shape[0], SQL), 1)
    high, low = high.astype(F32), low.astype(F32)
    return jnp.where(lane == 0, high, jnp.where(lane == 1, low, 0.0)).astype(BF)


def latent_kernel(where_to, resin_ref, gain_ref, down_ref, placed_ref, *refs):
    count = len(where_to)
    ins = refs[:count]
    res_ref, same_ref, other_ref = refs[count:]
    done = set()
    for (r0, c0), ref in zip(where_to, ins):
        at = (slice(r0, r0 + ref.shape[0]), slice(c0, c0 + ref.shape[1]))
        value = ref[...].astype(F32)
        if (r0, c0) in done:
            res_ref[at] += value
        else:
            res_ref[at] = value + resin_ref[at].astype(F32)
            done.add((r0, c0))
    residual = res_ref[...]
    placed = placed_ref[...]
    scaled = dot(placed, (residual * gain_ref[...]).astype(BF)).astype(BF)
    squares = jnp.sum(residual * residual, axis=1, keepdims=True)
    squares = dot(placed, squares_block(squares)).astype(BF)
    lat = down_ref.shape[1]
    mine, other = by_core(dot(scaled, down_ref[...]))
    same_ref[:, :lat] = mine.astype(BF)
    other_ref[:, :lat] = other.astype(BF)
    mine, other = by_core(squares)
    same_ref[:, lat:] = mine
    other_ref[:, lat:] = other


def add_up(ins, total):
    lat = total.shape[1] - SQL
    total[:, :lat] = sum(ref[:, :lat].astype(F32) for ref in ins).astype(BF)
    squares = sum(ref[:, lat:].astype(F32) for ref in ins)
    total[:, lat:] = squares_block(squares[:, 0:1] + squares[:, 1:2])


def merge_kernel(own_ref, recv_ref, out_ref):
    add_up((own_ref, recv_ref), out_ref)


def dispatch_kernel(n, count, *refs):
    ins, outs, total = refs[:count], refs[count : count + n], refs[count + n]
    c = lax.axis_index("ctx")
    rows = outs[0].shape[0]
    add_up(ins, total)
    for k in range(n):
        start = pl.multiple_of((c ^ k) * rows, rows)
        outs[k][...] = total[pl.ds(start, rows), :]


def expert_kernel(n, per, features, *refs):
    ins = refs[:n]
    kept_ref, taken_ref = refs[n : n + 2]
    outs = refs[n + 2 :]
    lat = outs[0].shape[1]
    contract = (((1,), (1,)), ((), ()))
    for j in range(per):
        rows = jnp.concatenate([ref[j * CAP : (j + 1) * CAP, :] for ref in ins], axis=0)
        square = rows[:, lat : lat + 1].astype(F32) + rows[:, lat + 1 : lat + 2].astype(F32)
        rows = (rows[:, :lat].astype(F32) * lax.rsqrt(square / features + EPS)).astype(BF)
        result = None
        for ref in (kept_ref, taken_ref):
            up, down = ref[j], ref[per + j]
            hidden = lax.dot_general(rows, up, contract, preferred_element_type=F32)
            hidden = jnp.maximum(hidden, 0.0)
            part = dot((hidden * hidden).astype(BF), down)
            result = part if result is None else result + part
        result = result.astype(BF)
        for k in range(n):
            outs[k][j * CAP : (j + 1) * CAP, :] = result[k * CAP : (k + 1) * CAP, :]


def share_kernel(per, up_ref, down_ref, kept_ref, given_ref, sem):
    core = lax.rem(lax.axis_index("heads"), 2)
    copies = []
    for i, ref in enumerate((up_ref, down_ref)):
        for k, (start, out) in enumerate(((core * per, kept_ref), ((1 - core) * per, given_ref))):
            copies.append(
                pltpu.make_async_copy(
                    ref.at[pl.ds(start, per)], out.at[pl.ds(i * per, per)], sem.at[2 * i + k]
                )
            )
    for copy in copies:
        copy.start()
    for copy in copies:
        copy.wait()


def share_experts(per, up, down):
    return pl.pallas_call(
        functools.partial(share_kernel, per),
        in_specs=[pl.BlockSpec(memory_space=pl.ANY)] * 2,
        out_specs=[VM] * 2,
        out_shape=[sds((2 * per, *up.shape[1:]))] * 2,
        scratch_shapes=[pltpu.SemaphoreType.DMA((4,))],
        compiler_params=pltpu.CompilerParams(vmem_limit_bytes=LIMIT),
        name="share",
    )(up, down)


def returned_kernel(n, *refs):
    ins, out_ref = refs[:n], refs[n]
    c = lax.axis_index("ctx")
    rows = ins[0].shape[0]
    for k in range(n):
        out_ref[pl.ds(pl.multiple_of((c ^ k) * rows, rows), rows), :] = ins[k][...]


def sum_kernel(*refs):
    refs[-1][...] = sum(ref[...].astype(F32) for ref in refs[:-1]).astype(BF)


def combine_kernel(mine_ref, other_ref, table_ref, res_ref, up_ref, out_ref):
    mine, other = mine_ref[...], other_ref[...]
    first = lax.rem(lax.axis_index("heads"), 2) == 0
    table = table_ref[...]
    half = table.shape[1] // 2
    combined = dot(table[:, :half], jnp.where(first, mine, other))
    combined = combined + dot(table[:, half:], jnp.where(first, other, mine))
    out_ref[...] = (res_ref[...] + dot(combined.astype(BF), up_ref[...])).astype(BF)


def local(
    ssm_input,
    decay_log,
    state_write,
    state_read,
    skip_scale,
    gate_input,
    ssm_gain,
    out_weight,
    residual_in,
    moe_gain,
    down_latent,
    expert_up,
    expert_down,
    up_latent,
    expert_ids,
    combine_fixed,
):
    n, nh = lax.axis_size("ctx"), lax.axis_size("heads")
    nx, ny = nh // 2, lax.axis_size("groups")
    both = ("ctx", "heads")
    rows, cols = ssm_input.shape
    heads = decay_log.shape[1]
    width = cols // heads
    size = state_write.shape[1]
    groups = cols // GRP
    piece = cols // n
    feats = residual_in.shape[1]
    owned = expert_up.shape[0]
    per = owned // 2
    slots = owned * n * CAP
    lat = down_latent.shape[1]
    swap = [(i, i ^ 1) for i in range(nh)]

    def exchange(arrays, senders=range(n), receivers=range(n)):
        out = [arrays[0]]
        for k in range(1, n):
            perm = [(i, i ^ k) for i in senders if i ^ k in receivers]
            out.append(lax.ppermute(arrays[k], "ctx", perm))
        return out

    def across(a):
        out = [a]
        for k in range(1, nx):
            out.append(lax.ppermute(a, "heads", [(i, i ^ (2 * k)) for i in range(nh)]))
        return out

    plan = plan_of(out_weight.shape[0], ny)
    chunks = cut(out_weight, pltpu.HBM, plan, range(1))
    chunks = chunks + cut(out_weight, pltpu.HBM, plan, range(1, len(plan)))
    far = [[] for _ in range(ny)]
    for j, chunk in enumerate(chunks):
        far[0].append(lax.ppermute(chunk, "ctx", [(0, 1), (n - 1, n - 2)]))
        for k in range(1, ny if j < len(plan) - 1 else 1):
            perm = []
            for y in range(ny):
                perm += [(y * n + c, (y ^ k) * n + c) for c in (1, n - 2)]
            far[k].append(lax.ppermute(far[0][j], ("groups", "ctx"), perm))

    outs = call(
        functools.partial(state_kernel, n, heads, width),
        [ssm_input, decay_log.T, state_write, skip_scale[None, :]],
        [sds((rows, cols), F32), sds((heads, rows), F32), sds((1, cols), F32)]
        + [sds((size + PAD, piece))] * n,
        [pltpu.VMEM((n, size + PAD, piece), BF)],
    )
    cume, cumt, skip, sends = outs[0], outs[1], outs[2], outs[3:]
    got = exchange(sends, senders=range(n - 1))
    count = min(heads // groups, 8)
    base = []
    for g in range(groups):
        steps = heads // groups // count
        base += call(
            functools.partial(within_kernel, g * steps, steps, count, width),
            [ssm_input, cume, cumt, state_write, state_read, skip],
            [sds((rows, GRP), F32)],
        )
    prior = call(
        functools.partial(prefix_kernel, n),
        got,
        [sds((size, piece))] * n,
        [pltpu.VMEM((n, size + PAD, piece), BF), pltpu.VMEM((n, size, piece), BF)],
    )
    prior = exchange(prior, receivers=range(1, n))
    placed, table = call(
        functools.partial(route_kernel, n, owned),
        [expert_ids.T, combine_fixed.T],
        [sds((slots, rows)), sds((rows, slots))],
    )
    per_group = GRP // piece
    normed = []
    for g in range(groups):
        normed += call(
            functools.partial(gate_kernel, n, g * per_group, per_group),
            [base[g], cume, gate_input, ssm_gain[None, :], state_read, *prior],
            [sds((rows, GRP))],
            [pltpu.VMEM((n, size, piece), BF)],
        )

    kept, given = share_experts(per, jnp.swapaxes(expert_up, 1, 2), expert_down)
    taken = lax.ppermute(given, "heads", swap)

    table_of = tasks(n)
    blocks = {("O", 0): normed}
    feat_block = out_weight.shape[1]
    ratio = n // nh
    got, where_to = [], []

    right = left = normed
    for s in range(1, n - 1):
        for name, line, perm in (
            ("R", right, [(i, i + 1) for i in range(s - 1, n - 1)]),
            ("L", left, [(i, i - 1) for i in range(1, n - s + 1)]),
        ):
            out = []
            for a in line:
                out.append(lax.ppermute(a, "ctx", perm))
            blocks[name, s] = out
        right, left = blocks["R", s], blocks["L", s]

    def options(slot_of_core):
        keys, choice = [], []
        for i in range(2 * n):
            task = table_of[i // 2][slot_of_core(i % 2)]
            if task is None:
                choice.append(0)
                continue
            if task[:2] not in keys:
                keys.append(task[:2])
            choice.append(keys.index(task[:2]))
        return tuple(choice), [blocks[k] for k in keys]

    def rest(held, entries):
        for xi in range(nx):
            for rr in range(ratio):
                perm = [
                    (cc * nh + 2 * xi + core, to * nh + f // ratio)
                    for cc, core, f, to in entries
                    if f % ratio == rr
                ]
                if perm:
                    got.append(lax.ppermute(held, both, perm))
                    where_to.append((0, rr * feat_block))

    def entries_of(slot_of_core, cores):
        return [
            (cc, k, cc, table_of[cc][slot_of_core(k)][2])
            for cc in range(n)
            for k in cores
            if table_of[cc][slot_of_core(k)] is not None
        ]

    for p in range((n - 2) // 2):
        choice, cands = options(lambda k: 2 * p + 1 - k)
        (sent,) = project(choice, cands, out_weight, None, 1)
        recv = lax.ppermute(sent, "heads", swap)
        choice, cands = options(lambda k: 2 * p + k)
        (held,) = project(choice, cands, out_weight, recv, 1)
        rest(held, entries_of(lambda k: 2 * p + k, (0, 1)))
    for i, keeper in ((n - 2, 0), (n - 1, 1)):
        choice, cands = options(lambda k: i)
        (own,) = project(choice, cands, out_weight, None, 1)
        recv = lax.ppermute(own, "heads", swap)
        (held,) = fold(own, recv, 1)
        rest(held, entries_of(lambda k: i, (keeper,)))
    choice, cands = options(lambda k: n - 1)
    (own,) = project_far(choice, cands, far)
    perm = [(c * nh + i, c * nh + i - 1) for c in (1, n - 2) for i in range(1, nh, 2)]
    recv = lax.ppermute(own, both, perm)
    (held,) = fold(own, recv, 1)
    rest(held, [(1, 0, 0, n - 1), (n - 2, 0, n - 1, 0)])

    wide = lat + SQL
    residual, same, apart = call(
        functools.partial(latent_kernel, tuple(where_to)),
        [residual_in, moe_gain[None, :], down_latent, placed, *got],
        [sds((rows, feats), F32), sds((slots // 2, wide)), sds((slots // 2, wide))],
    )
    recv = lax.ppermute(apart, "heads", swap)
    (total,) = call(merge_kernel, [same, recv], [sds((slots // 2, wide))])
    sends = call(
        functools.partial(dispatch_kernel, n, nx),
        across(total),
        [sds((per * CAP, wide))] * n,
        [pltpu.VMEM((slots // 2, wide), BF)],
    )
    sends = call(
        functools.partial(expert_kernel, n, per, float(feats * nh)),
        [*exchange(sends), kept, taken],
        [sds((per * CAP, lat))] * n,
    )
    (mine,) = call(functools.partial(returned_kernel, n), exchange(sends), [sds((slots // 2, lat))])
    (mine,) = call(sum_kernel, across(mine), [sds((slots // 2, lat))])
    other = lax.ppermute(mine, "heads", swap)
    (out,) = call(
        combine_kernel,
        [mine, other, table, residual, up_latent],
        [jax.ShapeDtypeStruct((rows, feats), BF)],
    )
    return out


def solution(mesh):
    placed = (
        P(("groups", "ctx"), "heads"),
        P(("groups", "ctx"), "heads"),
        P(("groups", "ctx"), None),
        P(("groups", "ctx"), None),
        P("heads"),
        P(("groups", "ctx"), "heads"),
        P("heads"),
        P("heads", "ctx"),
        P(("groups", "ctx"), "heads"),
        P("heads"),
        P("heads", None),
        P("ctx", None, "heads"),
        P("ctx", "heads", None),
        P(None, "heads"),
        P(("groups", "ctx"), None),
        P(("groups", "ctx"), None),
    )
    return jax.shard_map(
        local, mesh=mesh, in_specs=placed, out_specs=P(("groups", "ctx"), "heads"), check_vma=False
    )
```
